256 devices in a mesh: row: 32 (over y, x, core), col: 8 (over z).
Axes of the slice: x: 4, y: 4, z: 8, core: 2. Of those that a mesh axis runs over, the one named last changes fastest.
Arguments:
- features: bfloat16 [32768, 512], P(('row', 'col')), may hold values from -6 to 6
- tile_data: bfloat16 [256, 32, 2, 128, 128], P('row', 'col'), as said below
- tile_ids: int32 [256, 32, 2], P('row', 'col'), may hold values from 0 to 7, as said below
- tile_counts: int32 [256, 32], P('row', 'col'), may hold values from 0 to 2, as said below
- hist_tiles: bfloat16 [256, 8, 128, 128], P('row', 'col'), may hold values from -0.1875 to 0.1875
- hist_ids: int32 [256, 8], P('row', 'col'), may hold values from 0 to 31
- hist_cache: bfloat16 [4096, 512], P('col'), may hold values from -6 to 6
- first_weight: bfloat16 [512, 512], replicated, may hold values from -0.25 to 0.25
- second_weight: bfloat16 [512, 512], replicated, may hold values from -0.25 to 0.25
- grad_out: bfloat16 [32768, 512], P(('row', 'col')), may hold values from -6 to 6
Outputs:
- embedding: bfloat16 [32768, 512], P(('row', 'col'))
- grad_first: float32 [512, 512], replicated
- grad_second: float32 [512, 512], replicated
The draws below stay inside these ranges and needn't reach their ends.
Inputs may be any that keep to these rules, and one draw needn't show every extreme that they name: tile_ids[p, j, t] is a tile column within panel j; slots t >= tile_counts[p, j] are padding and must be ignored; the used slots of a tile row and panel name distinct columns; the matrix that the tiles describe is symmetric. `tile_counts`: the count depends only on the block row of the tile row and on the panel. `tile_data`: padded slots hold arbitrary values.
All inputs are finite; a program needn't handle non-finite values.
Results may differ from the reference program's by a relative error of at most 0.018.
Values may be sent and summed in bfloat16 or wider, within the bound.
No kernel may reach another device: no remote copies, remote signals or barrier semaphores. Data moves between devices by JAX's collectives and lax.ppermute only.
A program may use at most 128 MiB of HBM per device.

```python
import math
import jax
import jax.numpy as jnp
from jax import lax

F = 512
TILE = 128
TROWS = 8
MAXT = 2
PANELS = 32
SPLITS = 8
NB = 256
NODES = 32768
HBLK = 32


def tile_structure(key):
    base_key = jax.random.fold_in(key, 11)
    key_rows, key_pairs, key_shift, key_perm = jax.random.split(base_key, 4)
    weight_rows = jax.random.randint(key_rows, (PANELS,), 1, 4)
    upper_pairs = jax.random.randint(key_pairs, (PANELS, PANELS), 0, 4)
    row_grid = jnp.arange(PANELS)[:, None]
    col_grid = jnp.arange(PANELS)[None, :]
    upper_pairs = jnp.where(row_grid < col_grid, upper_pairs, upper_pairs.T)
    pair_counts = jnp.minimum(weight_rows[:, None] * weight_rows[None, :] * upper_pairs // 2, MAXT)
    diag_count = MAXT - 1 + MAXT % 2
    pair_counts = jnp.where(row_grid == col_grid, diag_count, pair_counts)
    first_pair = (row_grid == 0) & (col_grid == 1) | (row_grid == 1) & (col_grid == 0)
    pair_counts = jnp.where(first_pair, MAXT, pair_counts)
    raw_shift = jax.random.randint(key_shift, (PANELS, PANELS), 0, TROWS)
    lower_shift = jnp.mod(-(raw_shift.T + pair_counts.T - 1), TROWS)
    diag_shift = jnp.mod(-((diag_count - 1) // 2), TROWS)
    shifts = jnp.where(row_grid < col_grid, raw_shift, jnp.where(row_grid > col_grid, lower_shift, diag_shift))
    perm_keys = jax.random.split(key_perm, PANELS)
    orders = jax.vmap(lambda one_key: jax.random.permutation(one_key, TROWS))(perm_keys)
    inverse = jnp.argsort(orders, axis=1)
    slot_index = jnp.arange(MAXT)
    position = jnp.mod(orders[:, :, None, None] + shifts[:, None, :, None] + slot_index[None, None, None, :], TROWS)
    panel_grid = jnp.arange(PANELS)[None, None, :, None]
    picked_ids = inverse[panel_grid, position]
    return (picked_ids.reshape(NB, PANELS, MAXT).astype(jnp.int32), pair_counts.astype(jnp.int32))


def draw_tile_ids(key, part):
    picked_ids, pair_counts = tile_structure(key)
    return picked_ids


def draw_tile_counts(key, part):
    picked_ids, pair_counts = tile_structure(key)
    return jnp.repeat(pair_counts, TROWS, axis=0)


def draw_tile_data(key, part):
    picked_ids, pair_counts = tile_structure(key)
    factors = jax.random.normal(jax.random.fold_in(key, 23), (NB, TILE, TILE), jnp.float32)
    scale_value = (TILE * MAXT * PANELS) ** (-0.5)

    def one_row(row_index):
        tile_cols = jnp.arange(PANELS)[:, None] * TROWS + picked_ids[row_index]
        row_factor = factors[row_index]
        col_factor = factors[tile_cols]
        values = row_factor[None, None] * jnp.swapaxes(col_factor, 2, 3) + col_factor * row_factor.T[None, None]
        return values * scale_value
    return lax.map(one_row, jnp.arange(NB)).astype(jnp.bfloat16)


def with_ends(drawn, rng, low, largest):
    longest = drawn.shape.index(max(drawn.shape))
    spots = []
    for shift in (0, 1):
        where = [jax.random.randint(jax.random.fold_in(rng, axis), (), 0, length) for axis, length in enumerate(drawn.shape)]
        where[longest] = (where[longest] + shift) % drawn.shape[longest]
        spots.append(tuple(where))
    return drawn.at[spots[0]].set(low).at[spots[1]].set(largest)


def shard_levels(stream_key, extent, cuts, smallest, top_value):
    gain = 1.0
    for dim, blocks in cuts:
        steps = jax.random.uniform(jax.random.fold_in(jax.random.fold_in(stream_key, 6), dim), (blocks,), jnp.float32, smallest / len(cuts), top_value / len(cuts))
        gain = gain * jnp.repeat(jnp.exp(steps), extent[dim] // blocks).reshape((-1,) + (1,) * (len(extent) - 1 - dim))
    return gain


def bell_draw(own_key, dims, scale, bound, shards=(), dtype=jnp.bfloat16):
    entries = jax.random.normal(own_key, dims, jnp.float32) * scale
    if len(shards) > 0:
        entries = shard_levels(own_key, dims, shards, -0.22, 0.18) * entries
    return jnp.clip(entries, min=-bound, max=bound).astype(dtype)


def setup_inputs(seed: int = 0) -> dict:
    key_list = jax.random.split(jax.random.key(seed), 11)
    features = bell_draw(key_list[0], (NODES, F), 1.0, 6.0, ((0, 256),))
    tile_data = draw_tile_data(jax.random.fold_in(key_list[10], 71), 0)
    tile_ids = draw_tile_ids(jax.random.fold_in(key_list[10], 71), 0)
    tile_counts = draw_tile_counts(jax.random.fold_in(key_list[10], 71), 0)
    hist_tiles = bell_draw(key_list[4], (NB, SPLITS, TILE, TILE), (TILE * SPLITS) ** -0.5, 0.1875, ((0, 32), (1, 8)))
    hist_ids = with_ends(jax.random.randint(key_list[5], (NB, SPLITS), 0, HBLK), jax.random.fold_in(key_list[5], 1), 0, HBLK - 1).astype(jnp.int32)
    hist_cache = bell_draw(key_list[6], (HBLK * TILE, F), 1.0, 6.0, ((0, 8),))
    first_weight = bell_draw(key_list[7], (F, F), F ** -0.5, 0.25)
    second_weight = bell_draw(key_list[8], (F, F), F ** -0.5, 0.25)
    grad_out = bell_draw(key_list[9], (NODES, F), 1.0, 6.0, ((0, 256),))
    return {"features": features, "tile_data": tile_data, "tile_ids": tile_ids, "tile_counts": tile_counts, "hist_tiles": hist_tiles, "hist_ids": hist_ids, "hist_cache": hist_cache, "first_weight": first_weight, "second_weight": second_weight, "grad_out": grad_out}


def spread(source, tile_data, tile_ids, tile_counts):
    blocks = source.reshape(PANELS, TROWS, TILE, F)
    panel_index = jnp.arange(PANELS)[:, None]
    slot_index = jnp.arange(MAXT)[None, :]

    def one_row(row_index):
        chosen = blocks[panel_index, tile_ids[row_index]].astype(jnp.float32)
        keep_mask = (slot_index < tile_counts[row_index][:, None]).astype(jnp.float32)
        masked = tile_data[row_index].astype(jnp.float32) * keep_mask[:, :, None, None]
        return jnp.einsum('jtik,jtkf->if', masked, chosen)
    rows_out = lax.map(one_row, jnp.arange(TROWS * PANELS))
    return rows_out.reshape(TILE * TROWS * PANELS, F)

def history_term(hist_tiles, hist_ids, hist_cache):
    cache_blocks = hist_cache.reshape(HBLK, TILE, F)

    def one_row(row_index):
        chosen = cache_blocks[hist_ids[row_index]].astype(jnp.float32)
        return jnp.einsum('hik,hkf->if', hist_tiles[row_index].astype(jnp.float32), chosen)
    rows_out = lax.map(one_row, jnp.arange(TROWS * PANELS))
    return rows_out.reshape(TILE * TROWS * PANELS, F)

def reference(features, tile_data, tile_ids, tile_counts, hist_tiles, hist_ids, hist_cache, first_weight, second_weight, grad_out):
    first_agg = spread(features, tile_data, tile_ids, tile_counts).astype(jnp.bfloat16)
    first_pre = jnp.dot(first_agg, first_weight, preferred_element_type=jnp.float32)
    hidden = jax.nn.silu(first_pre).astype(jnp.bfloat16)
    history = history_term(hist_tiles, hist_ids, hist_cache)
    second_agg = (spread(hidden, tile_data, tile_ids, tile_counts) + history).astype(jnp.bfloat16)
    embedding = jnp.dot(second_agg, second_weight, preferred_element_type=jnp.float32).astype(jnp.bfloat16)
    grad_agg = jnp.dot(grad_out, second_weight.T, preferred_element_type=jnp.float32).astype(jnp.bfloat16)
    scale_value = 1.0 / math.sqrt(NODES)
    grad_second = jnp.dot(second_agg.T, grad_out, preferred_element_type=jnp.float32) * scale_value
    grad_hidden = spread(grad_agg, tile_data, tile_ids, tile_counts).astype(jnp.bfloat16)
    sigmoid_gate = jax.nn.sigmoid(first_pre)
    grad_pre = (grad_hidden.astype(jnp.float32) * sigmoid_gate * (1.0 + first_pre * (1.0 - sigmoid_gate))).astype(jnp.bfloat16)
    grad_first = jnp.dot(first_agg.T, grad_pre, preferred_element_type=jnp.float32) * scale_value
    return (embedding, grad_first, grad_second)
```

```python
import functools
import math

import jax
import jax.numpy as jnp
from jax import lax
from jax.experimental import pallas as pl
from jax.experimental.pallas import tpu as pltpu
from jax.sharding import Mesh, PartitionSpec as P

BF = jnp.bfloat16
F32 = jnp.float32
TILE = 128
VMEM = pl.BlockSpec(memory_space=pltpu.VMEM)
SMEM = pl.BlockSpec(memory_space=pltpu.SMEM)
ROWS = (((0,), (0,)), ((), ()))


def back_kernel(ids, counts, tiles, source, out, total):
    rows, panels, slots = tiles.shape[:3]
    width = total.shape[0] // panels // TILE
    total[...] = jnp.zeros_like(total)

    def one_row(p, carry):
        block = source[pl.ds(pl.multiple_of(p * TILE, TILE), TILE), :]
        for j in range(panels):
            used = counts[p, j]
            for t in range(slots):

                @pl.when(t < used)
                def _():
                    column = j * width + ids[p, j, t]
                    at = pl.ds(pl.multiple_of(column * TILE, TILE), TILE)
                    total[at, :] += lax.dot_general(
                        tiles[p, j, t], block, ROWS, preferred_element_type=F32
                    )

        return carry

    lax.fori_loop(0, rows, one_row, 0)
    out[...] = total[...].astype(out.dtype)


def back_product(ids, counts, tiles, source):
    rows, panels, slots = tiles.shape[:3]
    height = panels * 8 * TILE
    width = source.shape[1]
    return pl.pallas_call(
        back_kernel,
        out_shape=jax.ShapeDtypeStruct((height, width), BF),
        in_specs=[SMEM, SMEM, VMEM, VMEM],
        out_specs=VMEM,
        scratch_shapes=[pltpu.VMEM((height, width), F32)],
        compiler_params=pltpu.CompilerParams(vmem_limit_bytes=40 << 20),
        cost_estimate=pl.CostEstimate(
            flops=2 * rows * panels * slots * TILE * TILE * width,
            bytes_accessed=12 << 20,
            transcendentals=0,
        ),
        name="back_product",
    )(ids, counts, tiles, source)


def row_kernel(base, ids, counts, tiles, source, out):
    rows = out.shape[0] // TILE
    panels, slots = tiles.shape[1:3]
    width = source.shape[0] // panels // TILE

    def one_row(i, carry):
        p = base[0] + i
        acc = jnp.zeros((TILE, out.shape[1]), F32)
        for j in range(panels):
            used = counts[p, j]
            for t in range(slots):
                tile = tiles[p, j, t]
                tile = jnp.where(t < used, tile, jnp.zeros_like(tile))
                at = pl.multiple_of((j * width + ids[p, j, t]) * TILE, TILE)
                acc += jnp.dot(tile, source[pl.ds(at, TILE), :], preferred_element_type=F32)
        out[pl.ds(pl.multiple_of(i * TILE, TILE), TILE), :] = acc.astype(out.dtype)
        return carry

    lax.fori_loop(0, rows, one_row, 0)


def row_product(base, ids, counts, tiles, source, rows, dtype):
    panels, slots = tiles.shape[1:3]
    width = source.shape[1]
    return pl.pallas_call(
        row_kernel,
        out_shape=jax.ShapeDtypeStruct((rows * TILE, width), dtype),
        in_specs=[SMEM, SMEM, SMEM, VMEM, VMEM],
        out_specs=VMEM,
        compiler_params=pltpu.CompilerParams(vmem_limit_bytes=40 << 20),
        cost_estimate=pl.CostEstimate(
            flops=2 * rows * panels * slots * TILE * TILE * width,
            bytes_accessed=6 << 20,
            transcendentals=0,
        ),
        name="row_product",
    )(base, ids, counts, tiles, source)


def hist_kernel(place, ids, tiles, cache, out):
    splits, rows = tiles.shape[:2]
    blocks = cache.shape[0] // TILE
    first = place[0] * blocks

    def one_row(p, carry):
        at = pl.ds(pl.multiple_of(p * TILE, TILE), TILE)
        out[at, :] = jnp.zeros((TILE, out.shape[1]), F32)
        for q in range(splits):
            block = ids[q, p] - first

            @pl.when((block >= 0) & (block < blocks))
            def _():
                part = cache[pl.ds(pl.multiple_of(block * TILE, TILE), TILE), :]
                out[at, :] += jnp.dot(tiles[q, p], part, preferred_element_type=F32)

        return carry

    lax.fori_loop(0, rows, one_row, 0)


def hist_product(place, ids, tiles, cache):
    splits, rows = tiles.shape[:2]
    width = cache.shape[1]
    return pl.pallas_call(
        hist_kernel,
        out_shape=jax.ShapeDtypeStruct((rows * TILE, width), F32),
        in_specs=[SMEM, SMEM, VMEM, VMEM],
        out_specs=VMEM,
        compiler_params=pltpu.CompilerParams(vmem_limit_bytes=40 << 20),
        cost_estimate=pl.CostEstimate(
            flops=2 * rows * splits * TILE * TILE * width,
            bytes_accessed=5 << 20,
            transcendentals=0,
        ),
        name="hist_product",
    )(place, ids, tiles, cache)


def local(
    sizes,
    features,
    tile_data,
    tile_ids,
    tile_counts,
    hist_tiles,
    hist_ids,
    hist_cache,
    first_weight,
    second_weight,
    grad_out,
):
    chips, depth, everyone = sizes
    share, width = features.shape
    node_count = share * everyone
    scale = 1.0 / math.sqrt(node_count)
    core = lax.axis_index("core")
    place = lax.axis_index("z").astype(jnp.int32)[None]

    both = jnp.concatenate([features, grad_out], axis=1)
    pair_rows = lax.all_gather(both, ("core", "z"), axis=0, tiled=True)
    tiles = lax.all_to_all(tile_data, "core", split_axis=1, concat_axis=0, tiled=True)
    numbers = jnp.concatenate([tile_ids, tile_counts[:, :, None]], axis=2)
    numbers = lax.all_to_all(numbers, "core", split_axis=1, concat_axis=0, tiled=True)
    ids, counts = numbers[:, :, :2], numbers[:, :, 2]

    link_tiles = lax.all_gather(hist_tiles[:, 0], "z", axis=0)
    link_ids = lax.all_gather(hist_ids[:, 0], "z", axis=0)

    back = back_product(ids, counts, tiles, pair_rows)
    back = back.reshape(chips, share, 2 * width)
    back = lax.all_to_all(back, ("y", "x"), split_axis=0, concat_axis=0, tiled=True)
    summed = jnp.sum(back.astype(F32), axis=0).astype(BF)
    first_agg, grad_sum = summed[:, :width], summed[:, width:]

    first_pre = jnp.dot(first_agg, first_weight, preferred_element_type=F32)
    hidden = jax.nn.silu(first_pre).astype(BF)
    hidden_pair = lax.all_gather(hidden, ("y", "x"), axis=0, tiled=True)

    grad_hidden = lax.dot_general(
        grad_sum, second_weight, (((1,), (1,)), ((), ())), preferred_element_type=F32
    )
    gate = jax.nn.sigmoid(first_pre)
    grad_pre = (grad_hidden * gate * (1.0 + first_pre * (1.0 - gate))).astype(BF)
    history = hist_product(place, link_ids, link_tiles, hist_cache)
    own_grad = lax.dynamic_slice(
        pair_rows, (core * (share * depth), width), (share * depth, width)
    )
    first_term = lax.dot_general(first_agg, grad_pre, ROWS, preferred_element_type=F32)
    second_term = lax.dot_general(hidden, grad_sum, ROWS, preferred_element_type=F32)
    second_term += lax.dot_general(history.astype(BF), own_grad, ROWS, preferred_element_type=F32)
    terms = jnp.concatenate([first_term, second_term], axis=1).astype(BF)
    terms = terms.reshape(width // 16, 16, 2 * width // 128, 128).transpose(0, 2, 1, 3)
    terms = terms.reshape(everyone, 16, 128)
    terms = lax.all_to_all(terms, ("y", "x", "core", "z"), split_axis=0, concat_axis=0, tiled=True)
    term = (jnp.sum(terms.astype(F32), axis=0) * scale).astype(BF)
    spread = lax.all_to_all(
        jnp.broadcast_to(term[None], (everyone, 16, 128)),
        ("y", "x", "core", "z"),
        split_axis=0,
        concat_axis=0,
        tiled=True,
    )
    grads = spread.reshape(width // 16, 2 * width // 128, 16, 128).transpose(0, 2, 1, 3)
    grads = grads.reshape(width, 2 * width).astype(F32)

    rows = tile_data.shape[0]
    other = ((1 - core) * rows).astype(jnp.int32)[None]
    mine = (core * rows).astype(jnp.int32)[None]
    sent = row_product(other, ids, counts, tiles, hidden_pair, rows, BF)
    taken = lax.ppermute(sent, "core", [(0, 1), (1, 0)])
    kept = row_product(mine, ids, counts, tiles, hidden_pair, rows, F32)
    part = (kept + taken.astype(F32) + history).astype(BF).reshape(depth, share, width)
    part = lax.all_to_all(part, "z", split_axis=0, concat_axis=0, tiled=True)
    second_agg = jnp.sum(part.astype(F32), axis=0).astype(BF)
    embedding = jnp.dot(second_agg, second_weight, preferred_element_type=F32).astype(BF)
    return (embedding, grads[:, :width], grads[:, width:])


def solution(mesh):
    devices = mesh.devices.reshape(4, 4, 2, 8)
    chip_mesh = Mesh(devices, ("y", "x", "core", "z"))
    row = ("y", "x", "core")
    everything = ("y", "x", "core", "z")
    placed = (
        P(everything, None),
        P(row, "z", None, None, None),
        P(row, "z", None),
        P(row, "z"),
        P(row, "z", None, None),
        P(row, "z"),
        P("z", None),
        P(),
        P(),
        P(everything, None),
    )
    return jax.shard_map(
        functools.partial(local, (16, 8, 256)),
        mesh=chip_mesh,
        in_specs=placed,
        out_specs=(P(everything, None), P(), P()),
        check_vma=False,
    )
```

```python
import functools
import math

import jax
import jax.numpy as jnp
from jax import lax
from jax.experimental import pallas as pl
from jax.experimental.pallas import tpu as pltpu
from jax.sharding import Mesh, PartitionSpec as P

BF = jnp.bfloat16
F32 = jnp.float32
TILE = 128
VMEM = pl.BlockSpec(memory_space=pltpu.VMEM)
SMEM = pl.BlockSpec(memory_space=pltpu.SMEM)
ROWS = (((0,), (0,)), ((), ()))
COLS = (((1,), (1,)), ((), ()))
ROW = ("y", "x", "core")
ALL = ("y", "x", "core", "z")
SWAP = [(0, 1), (1, 0)]
RING = 8
SIDE = 4


def call(kernel, out_shape, specs, scratch, flops, moved, name):
    return pl.pallas_call(
        kernel,
        out_shape=out_shape,
        in_specs=specs,
        out_specs=jax.tree.map(lambda _: VMEM, out_shape),
        scratch_shapes=scratch,
        compiler_params=pltpu.CompilerParams(vmem_limit_bytes=40 << 20),
        cost_estimate=pl.CostEstimate(flops=flops, bytes_accessed=moved, transcendentals=0),
        name=name,
    )


def block_rows(index):
    return pl.ds(pl.multiple_of(index * TILE, TILE), TILE)


def ring_slot(source, mine):
    off = (source - mine + RING) % RING
    return jnp.where(off < RING // 2, 2 * off, 2 * RING - 1 - 2 * off)


def ring(x, whole):
    up = [(i, (i + 1) % RING) for i in range(RING)]
    down = [(i, (i - 1) % RING) for i in range(RING)]
    half = x.shape[0] // 2
    pieces, u, d = [x], x, x
    for _ in range(RING // 2 - 1):
        u, d = lax.ppermute(u, "z", up), lax.ppermute(d, "z", down)
        pieces += [u, d]
    pieces += [lax.ppermute(u[:half], "z", up), lax.ppermute(d[half:], "z", down)]
    return jnp.concatenate(pieces, axis=0) if whole else pieces


def back_sums(column, where, num_a, num_b, tile_a, tile_b, src_a, src_b, total):
    z, core = where[0], where[1]
    rows, panels, slots = tile_b.shape[:3]
    columns = total.shape[0] // panels // TILE
    lanes = pl.ds(column, total.shape[1])
    total[...] = jnp.zeros_like(total)
    for num, tiles, src, first in (
        (num_a, tile_a, src_a, panels * core),
        (num_b, tile_b, src_b, 0),
    ):

        def one_row(i, carry):
            block = src[block_rows(ring_slot(i, z)), lanes]
            parts = []
            for j in range(panels):
                used = num[i, first + j, slots]
                for t in range(slots):
                    tile = tiles[i, first + j, t]
                    tile = jnp.where(t < used, tile, jnp.zeros_like(tile))
                    part = lax.dot_general(tile, block, ROWS, preferred_element_type=F32)
                    parts.append((j * columns + num[i, first + j, t], part))
            for place, part in parts:
                total[block_rows(place), :] += part
            return carry

        lax.fori_loop(0, rows, one_row, 0)


def first_back_kernel(*refs):
    out, total = refs[-2:]
    back_sums(0, *refs[:-2], total)
    for a in range(SIDE):
        for b in range(SIDE):
            out[a, b] = total[pl.ds((a * SIDE + b) * TILE, TILE), :].astype(BF)


def second_back_kernel(*refs):
    outs, total = refs[7:-1], refs[-1]
    where = refs[0]
    back_sums(total.shape[1], *refs[:7], total)
    for s in range(SIDE):
        for t in range(SIDE):
            block = ((where[2] + t) % SIDE) * SIDE + (where[3] + s) % SIDE
            value = total[block_rows(block), :].astype(BF)
            if s == 0:
                outs[0][t] = value
            else:
                outs[2 * s - 1 + t // 2][t % 2] = value


def back_product(kernel, out_shape, *operands):
    rows, panels, slots = operands[4].shape[:3]
    height, width = panels * 8 * TILE, operands[5].shape[1] // 2
    return call(
        kernel,
        out_shape,
        [SMEM] * 3 + [VMEM] * 4,
        [pltpu.VMEM((height, width), F32)],
        4 * rows * panels * slots * TILE * TILE * width,
        8 << 20,
        "back_product",
    )(*operands)


def row_blocks(where, num, tiles, source, first, start, out):
    rows, _, slots = tiles.shape[:3]
    panels = 2
    columns = source.shape[0] // panels // TILE

    def one_row(i, carry):
        at = block_rows(i)
        acc = start[at, :] if start is not None else jnp.zeros((TILE, out.shape[1]), F32)
        for j in range(panels):
            used = num[i, first + j, slots]
            for t in range(slots):
                tile = tiles[i, first + j, t]
                tile = jnp.where(t < used, tile, jnp.zeros_like(tile))
                part = source[block_rows(j * columns + num[i, first + j, t]), :]
                acc += jnp.dot(tile, part, preferred_element_type=F32)
        out[at, :] = acc.astype(out.dtype)
        return carry

    lax.fori_loop(0, rows, one_row, 0, unroll=2)


def partner_kernel(where, num, tiles, *refs):
    pieces, (out, pair) = refs[:-2], refs[-2:]
    step = pieces[0].shape[0] // SIDE
    order = (0, -1, 1, 2)
    for half in range(2):
        group = pieces[5 * half : 5 * half + 5]
        for n, piece in enumerate(group):
            far = order[min(n, 3)]
            inner = order if n < 3 else order[2 * (n - 3) : 2 * (n - 3) + 2]
            for m, near in enumerate(inner):
                y, x = (near, far) if half == 0 else (far, near)
                block = ((where[2] + y) % SIDE) * SIDE + (where[3] + x) % SIDE
                at = pl.multiple_of(block * TILE + half * step, step)
                pair[pl.ds(at, step), :] = piece[m * step : (m + 1) * step, :]
    row_blocks(where, num, tiles, pair, 0, None, out)


def own_kernel(where, num, tiles, pair, history, out):
    row_blocks(where, num, tiles, pair, 2 * where[1], history, out)


def partner_product(where, num, tiles, pieces):
    rows, width = tiles.shape[0], pieces[0].shape[1]
    return call(
        partner_kernel,
        (
            jax.ShapeDtypeStruct((rows * TILE, width), BF),
            jax.ShapeDtypeStruct((2 * rows * TILE, width), BF),
        ),
        [SMEM] * 2 + [VMEM] * 11,
        [],
        8 * rows * TILE * TILE * width,
        5 << 20,
        "row_product",
    )(where, num, tiles, *pieces)


def own_product(where, num, tiles, pair, history):
    rows, width = tiles.shape[0], pair.shape[1]
    return call(
        own_kernel,
        jax.ShapeDtypeStruct((rows * TILE, width), F32),
        [SMEM] * 2 + [VMEM] * 3,
        [],
        8 * rows * TILE * TILE * width,
        5 << 20,
        "row_product",
    )(where, num, tiles, pair, history)


def hist_kernel(where, ids, cache, grads, *refs):
    pieces, (out, term) = refs[:-2], refs[-2:]
    blocks = cache.shape[0] // TILE
    z = where[0]
    rows = pieces[0].shape[0]
    out[...] = jnp.zeros_like(out)
    offsets = [0, -1, 1, -2, 2, -3, 3, 4, 4]
    start = 0
    for n, piece in enumerate(pieces):
        source = (z + offsets[n] + RING) % RING
        skip = rows // 2 if n == len(pieces) - 1 else 0

        def one_row(p, carry):
            block = ids[source, skip + p] - z * blocks

            @pl.when((block >= 0) & (block < blocks))
            def _():
                part = cache[block_rows(block), :]
                out[block_rows(skip + p), :] += jnp.dot(
                    piece[p], part, preferred_element_type=F32
                )

            return carry

        lax.fori_loop(0, piece.shape[0], one_row, 0)
    term[...] = jnp.zeros_like(term)

    def one_term(p, carry):
        term[...] += lax.dot_general(
            out[block_rows(p), :].astype(BF),
            grads[block_rows(ring_slot(p, z)), pl.ds(term.shape[1], term.shape[1])],
            ROWS,
            preferred_element_type=F32,
        )
        return carry

    lax.fori_loop(0, rows, one_term, 0)


def hist_product(where, ids, cache, grads, pieces):
    rows, width = pieces[0].shape[0], cache.shape[1]
    return call(
        hist_kernel,
        (
            jax.ShapeDtypeStruct((rows * TILE, width), F32),
            jax.ShapeDtypeStruct((width, width), F32),
        ),
        [SMEM] * 2 + [VMEM] * (2 + len(pieces)),
        [],
        2 * rows * TILE * TILE * width + 2 * rows * TILE * width * width,
        6 << 20,
        "hist_product",
    )(where, ids, cache, grads, *pieces)


def hidden_kernel(parts, weight, agg, pre, hidden, upper, lower):
    total = parts[0].astype(F32)
    for i in range(1, parts.shape[0]):
        total += parts[i].astype(F32)
    agg[...] = total.astype(BF)
    v = jnp.dot(agg[...], weight[...], preferred_element_type=F32)
    pre[...] = v
    h = (v * (1.0 / (1.0 + jnp.exp(-v)))).astype(BF)
    hidden[...] = h
    half = upper.shape[0]
    upper[...] = h[:half]
    lower[...] = h[half:]


def hidden_step(parts, weight):
    share, width = parts.shape[1:]
    return call(
        hidden_kernel,
        (
            jax.ShapeDtypeStruct((share, width), BF),
            jax.ShapeDtypeStruct((share, width), F32),
            jax.ShapeDtypeStruct((share, width), BF),
            jax.ShapeDtypeStruct((share // 2, width), BF),
            jax.ShapeDtypeStruct((share // 2, width), BF),
        ),
        [VMEM] * 2,
        [],
        2 * share * width * width,
        4 << 20,
        "hidden_step",
    )(parts, weight)


def grads_kernel(own, up, down, agg, pre, hidden, weight, term, out):
    grad_sum = (own[...].astype(F32) + up[...].astype(F32) + down[...].astype(F32)).astype(BF)
    grad_hidden = lax.dot_general(grad_sum, weight[...], COLS, preferred_element_type=F32)
    v = pre[...]
    gate = 1.0 / (1.0 + jnp.exp(-v))
    grad_pre = (grad_hidden * gate * (1.0 + v * (1.0 - gate))).astype(BF)
    first = lax.dot_general(agg[...], grad_pre, ROWS, preferred_element_type=F32)
    second = lax.dot_general(hidden[...], grad_sum, ROWS, preferred_element_type=F32) + term[...]
    deep, wide = out.shape[2:]
    for n, value in enumerate((first, second)):
        value = value.astype(BF)
        for i in range(out.shape[0]):
            for s in range(out.shape[1] // 2):
                out[i, n * (out.shape[1] // 2) + s] = value[
                    i * deep : (i + 1) * deep, s * wide : (s + 1) * wide
                ]


def grads_step(own, up, down, agg, pre, hidden, weight, term):
    share, width = agg.shape
    return call(
        grads_kernel,
        jax.ShapeDtypeStruct((width // 16, 2 * width // 128, 16, 128), BF),
        [VMEM] * 8,
        [],
        6 * share * width * width,
        5 << 20,
        "grads_step",
    )(own, up, down, agg, pre, hidden, weight, term)


def swap_sum(x, axis):
    got = lax.all_to_all(x, axis, split_axis=0, concat_axis=0, tiled=True)
    return jnp.sum(got.astype(F32), axis=0)


def share_out(x, axis, n):
    many = jnp.broadcast_to(x[None], (n, *x.shape))
    return lax.all_to_all(many, axis, split_axis=0, concat_axis=0, tiled=True)


def hop(x, axis, n, step):
    return lax.ppermute(x, axis, [(i, (i + step) % n) for i in range(n)])


def side_gather(x, axis):
    half = x.shape[0] // 2
    p, m = hop(x, axis, SIDE, 1), hop(x, axis, SIDE, -1)
    return [x, p, m, hop(p[:half], axis, SIDE, 1), hop(m[half:], axis, SIDE, -1)]


def add(*terms):
    return sum(t.astype(F32) for t in terms).astype(BF)


def side_reduce(own, near, far, back, axis):
    u, d = hop(far[0], axis, SIDE, 1), hop(far[1], axis, SIDE, -1)
    still = hop(near[1], axis, SIDE, 1), hop(back[0], axis, SIDE, -1)
    near, back = hop(add(near[0], u), axis, SIDE, 1), hop(add(back[1], d), axis, SIDE, -1)
    return own, (near, still[0]), (still[1], back)


def ring_reduce(block, z):
    half = RING // 2
    top, low = block(half)
    rows = top.shape[0]
    up = hop(top.astype(BF), "z", RING, 1)
    down = hop(low.astype(BF), "z", RING, -1)
    for s in range(half - 1, 0, -1):
        top, low = block(s)
        if s == half - 1:
            up = jnp.concatenate([top + up.astype(F32), low], axis=0).astype(BF)
            top, low = block(-s)
            down = jnp.concatenate([top, low + down.astype(F32)], axis=0).astype(BF)
        else:
            up = (jnp.concatenate([top, low], axis=0) + up.astype(F32)).astype(BF)
            down = (jnp.concatenate(block(-s), axis=0) + down.astype(F32)).astype(BF)
        up, down = hop(up, "z", RING, 1), hop(down, "z", RING, -1)
    return add(jnp.concatenate(block(0), axis=0), up, down)


def local(
    everyone,
    features,
    tile_data,
    tile_ids,
    tile_counts,
    hist_tiles,
    hist_ids,
    hist_cache,
    first_weight,
    second_weight,
    grad_out,
):
    share, width = features.shape
    scale = 1.0 / math.sqrt(share * everyone)
    core = lax.axis_index("core").astype(jnp.int32)
    z = lax.axis_index("z").astype(jnp.int32)
    y, x = (lax.axis_index(a).astype(jnp.int32) for a in ("y", "x"))
    where = jnp.stack([z, core, y, x])
    rows, panels = tile_data.shape[:2]

    numbers = jnp.concatenate([tile_ids, tile_counts[:, :, None]], axis=2)
    away = (1 - core) * (panels // 2)
    num_b = lax.ppermute(
        lax.dynamic_slice_in_dim(numbers, away, panels // 2, axis=1), "core", SWAP
    )
    tile_b = lax.ppermute(
        lax.dynamic_slice_in_dim(tile_data, away, panels // 2, axis=1), "core", SWAP
    )
    link_ids = share_out(hist_ids[:, 0], "z", RING)

    rows_a = ring(jnp.concatenate([features, grad_out], axis=1), True)
    rows_b = lax.ppermute(rows_a, "core", SWAP)
    operands = where, numbers, num_b, tile_data, tile_b, rows_a, rows_b
    first = back_product(
        first_back_kernel, jax.ShapeDtypeStruct((SIDE, SIDE, TILE, width), BF), *operands
    )
    first = swap_sum(first, "y").astype(BF)
    first = lax.all_to_all(first, "x", split_axis=0, concat_axis=0, tiled=True)
    shapes = [(SIDE, TILE, width)] + [(SIDE // 2, TILE, width)] * 6
    own, *rest = back_product(
        second_back_kernel, tuple(jax.ShapeDtypeStruct(s, BF) for s in shapes), *operands
    )
    own, up, down = side_reduce(own, rest[:2], rest[2:4], rest[4:], "x")
    half = SIDE // 2
    blocks = [add(own[t], up[t // half][t % half], down[t // half][t % half]) for t in range(SIDE)]
    cuts = [(b[: share // 2], b[share // 2 :]) for b in blocks[1:]]
    own, up, down = side_reduce(blocks[0], *cuts, "y")

    links = ring(hist_tiles[:, 0], False)
    history, hist_term = hist_product(where, link_ids, hist_cache, rows_a, links)

    first_agg, first_pre, hidden, upper, lower = hidden_step(first, first_weight)
    upper = side_gather(jnp.concatenate(side_gather(upper, "y"), axis=0), "x")
    lower = side_gather(jnp.concatenate(side_gather(lower, "x"), axis=0), "y")

    up, down = jnp.concatenate(up, axis=0), jnp.concatenate(down, axis=0)
    terms = grads_step(own, up, down, first_agg, first_pre, hidden, second_weight, hist_term)
    terms = swap_sum(terms, ROW).astype(BF)
    term = (swap_sum(terms, "z") * scale).astype(BF)
    spread = share_out(share_out(term, "z", RING).reshape(RING, 16, 128), ROW, everyone // RING)
    grads = spread.reshape(width // 16, 2 * width // 128, 16, 128).transpose(0, 2, 1, 3)
    grads = grads.reshape(width, 2 * width).astype(F32)

    sent, pair = partner_product(where, num_b, tile_b, upper + lower)
    taken = lax.ppermute(sent, "core", SWAP)
    kept = own_product(where, numbers, tile_data, pair, history)

    def block(offset):
        at = ((z + offset) % RING) * share
        size = share // 2
        return [
            lax.dynamic_slice_in_dim(kept, at + n * size, size)
            + lax.dynamic_slice_in_dim(taken, at + n * size, size).astype(F32)
            for n in range(2)
        ]

    second_agg = ring_reduce(block, z)
    embedding = jnp.dot(second_agg, second_weight, preferred_element_type=F32).astype(BF)
    return (embedding, grads[:, :width], grads[:, width:])


def solution(mesh):
    chip_mesh = Mesh(mesh.devices.reshape(4, 4, 2, 8), ("y", "x", "core", "z"))
    placed = (
        P(ALL, None),
        P(ROW, "z", None, None, None),
        P(ROW, "z", None),
        P(ROW, "z"),
        P(ROW, "z", None, None),
        P(ROW, "z"),
        P("z", None),
        P(),
        P(),
        P(ALL, None),
    )
    return jax.shard_map(
        functools.partial(local, 256),
        mesh=chip_mesh,
        in_specs=placed,
        out_specs=(P(ALL, None), P(), P()),
        check_vma=False,
    )
```

```python
import functools
import math

import jax
import jax.numpy as jnp
from jax import lax
from jax.experimental import pallas as pl
from jax.experimental.pallas import tpu as pltpu
from jax.sharding import Mesh, PartitionSpec as P

BF = jnp.bfloat16
F32 = jnp.float32
TILE = 128
VMEM = pl.BlockSpec(memory_space=pltpu.VMEM)
SMEM = pl.BlockSpec(memory_space=pltpu.SMEM)
ROWS = (((0,), (0,)), ((), ()))
COLS = (((1,), (1,)), ((), ()))
ROW = ("y", "x", "core")
ALL = ("y", "x", "core", "z")
SWAP = [(0, 1), (1, 0)]
RING = 8
SIDE = 4


def call(kernel, out_shape, specs, scratch, flops, moved, name):
    return pl.pallas_call(
        kernel,
        out_shape=out_shape,
        in_specs=specs,
        out_specs=jax.tree.map(lambda _: VMEM, out_shape),
        scratch_shapes=scratch,
        compiler_params=pltpu.CompilerParams(vmem_limit_bytes=40 << 20),
        cost_estimate=pl.CostEstimate(flops=flops, bytes_accessed=moved, transcendentals=0),
        name=name,
    )


def block_rows(index):
    return pl.ds(pl.multiple_of(index * TILE, TILE), TILE)


def ring_slot(source, mine):
    off = (source - mine) & (RING - 1)
    return jnp.where(off < RING // 2, 2 * off, 2 * RING - 1 - 2 * off)


def ring(x):
    up = [(i, (i + 1) % RING) for i in range(RING)]
    down = [(i, (i - 1) % RING) for i in range(RING)]
    half = x.shape[0] // 2
    pieces, u, d = [x], x, x
    for _ in range(RING // 2 - 1):
        u, d = lax.ppermute(u, "z", up), lax.ppermute(d, "z", down)
        pieces += [u, d]
    pieces += [lax.ppermute(u[:half], "z", up), lax.ppermute(d[half:], "z", down)]
    return jnp.concatenate(pieces, axis=0)


def back_sums(column, where, num_a, num_b, tile_a, tile_b, src_a, src_b, total):
    z, core = where[0], where[1]
    rows, panels, slots = tile_b.shape[:3]
    columns = total.shape[0] // panels // TILE
    lanes = pl.ds(column, total.shape[1])
    total[...] = jnp.zeros_like(total)
    for num, tiles, src, first in (
        (num_a, tile_a, src_a, panels * core),
        (num_b, tile_b, src_b, 0),
    ):

        def one_row(i, carry):
            block = src[block_rows(ring_slot(i, z)), lanes]
            parts = []
            for j in range(panels):
                used = num[i, first + j, slots]
                for t in range(slots):
                    tile = tiles[i, first + j, t]
                    tile = jnp.where(t < used, tile, jnp.zeros_like(tile))
                    part = lax.dot_general(tile, block, ROWS, preferred_element_type=F32)
                    parts.append((j * columns + num[i, first + j, t], part))
            for place, part in parts:
                total[block_rows(place), :] += part
            return carry

        lax.fori_loop(0, rows, one_row, 0)


def first_back_kernel(*refs):
    out, total = refs[-2:]
    back_sums(0, *refs[:-2], total)
    for a in range(out.shape[0]):
        out[a] = total[pl.ds(a * TILE, TILE), :].astype(BF)


def second_back_kernel(*refs):
    outs, total = refs[7:-1], refs[-1]
    where = refs[0]
    back_sums(total.shape[1], *refs[:7], total)
    for s in range(SIDE):
        for t in range(SIDE):
            block = ((where[2] + t) & (SIDE - 1)) * SIDE + ((where[3] + s) & (SIDE - 1))
            outs[s][t] = total[block_rows(block), :].astype(BF)


def back_product(kernel, out_shape, *operands):
    rows, panels, slots = operands[4].shape[:3]
    height, width = panels * 8 * TILE, operands[5].shape[1] // 2
    return call(
        kernel,
        out_shape,
        [SMEM] * 3 + [VMEM] * 4,
        [pltpu.VMEM((height, width), F32)],
        4 * rows * panels * slots * TILE * TILE * width,
        8 << 20,
        "back_product",
    )(*operands)


def row_blocks(where, num, tiles, source, first, start, out):
    rows, _, slots = tiles.shape[:3]
    panels = 2
    columns = source.shape[0] // panels // TILE

    def one_row(i, carry):
        at = block_rows(i)
        acc = start[at, :] if start is not None else jnp.zeros((TILE, out.shape[1]), F32)
        for j in range(panels):
            used = num[i, first + j, slots]
            for t in range(slots):
                tile = tiles[i, first + j, t]
                tile = jnp.where(t < used, tile, jnp.zeros_like(tile))
                part = source[block_rows(j * columns + num[i, first + j, t]), :]
                acc += jnp.dot(tile, part, preferred_element_type=F32)
        out[at, :] = acc.astype(out.dtype)
        return carry

    lax.fori_loop(0, rows, one_row, 0, unroll=2)


def partner_kernel(where, num, tiles, pair, out):
    row_blocks(where, num, tiles, pair, 0, None, out)


def own_kernel(where, num, tiles, pair, history, out):
    row_blocks(where, num, tiles, pair, 2 * where[1], history, out)


def partner_product(where, num, tiles, pair):
    rows, width = tiles.shape[0], pair.shape[1]
    return call(
        partner_kernel,
        jax.ShapeDtypeStruct((rows * TILE, width), BF),
        [SMEM] * 2 + [VMEM] * 2,
        [],
        8 * rows * TILE * TILE * width,
        4 << 20,
        "row_product",
    )(where, num, tiles, pair)


def own_product(where, num, tiles, pair, history):
    rows, width = tiles.shape[0], pair.shape[1]
    return call(
        own_kernel,
        jax.ShapeDtypeStruct((rows * TILE, width), F32),
        [SMEM] * 2 + [VMEM] * 3,
        [],
        8 * rows * TILE * TILE * width,
        5 << 20,
        "row_product",
    )(where, num, tiles, pair, history)


def hist_kernel(where, ids, cache, grads, *refs):
    pieces, (out, term) = refs[:-2], refs[-2:]
    blocks = cache.shape[0] // TILE
    z = where[0]
    rows = ids.shape[1]
    out[...] = jnp.zeros_like(out)
    for n, piece in enumerate(pieces):

        def one_row(p, carry):
            block = ids[n, p] - z * blocks

            @pl.when((block >= 0) & (block < blocks))
            def _():
                out[block_rows(p), :] += jnp.dot(
                    piece[block_rows(p), :],
                    cache[block_rows(block), :],
                    preferred_element_type=F32,
                )

            return carry

        lax.fori_loop(0, rows, one_row, 0)
    term[...] = jnp.zeros_like(term)

    def one_term(p, carry):
        term[...] += lax.dot_general(
            out[block_rows(p), :].astype(BF),
            grads[block_rows(ring_slot(p, z)), pl.ds(term.shape[1], term.shape[1])],
            ROWS,
            preferred_element_type=F32,
        )
        return carry

    lax.fori_loop(0, rows, one_term, 0)


def hist_product(where, ids, cache, grads, pieces):
    rows, width = ids.shape[1], cache.shape[1]
    return call(
        hist_kernel,
        (
            jax.ShapeDtypeStruct((rows * TILE, width), F32),
            jax.ShapeDtypeStruct((width, width), F32),
        ),
        [SMEM] * 2 + [VMEM] * (2 + len(pieces)),
        [],
        2 * rows * TILE * TILE * width + 2 * rows * TILE * width * width,
        6 << 20,
        "hist_product",
    )(where, ids, cache, grads, *pieces)


def hidden_kernel(parts, weight, after, agg, pre, hidden):
    total = parts[0].astype(F32)
    for i in range(1, parts.shape[0]):
        total += parts[i].astype(F32)
    agg[...] = total.astype(BF)
    v = jnp.dot(agg[...], weight[...], preferred_element_type=F32)
    pre[...] = v
    h = (v * (1.0 / (1.0 + jnp.exp(-v)))).astype(BF)
    for i in range(hidden.shape[0]):
        hidden[i] = h


def hidden_step(parts, weight, after):
    share, width = parts.shape[1:]
    return call(
        hidden_kernel,
        (
            jax.ShapeDtypeStruct((share, width), BF),
            jax.ShapeDtypeStruct((share, width), F32),
            jax.ShapeDtypeStruct(parts.shape, BF),
        ),
        [VMEM] * 2 + [pl.BlockSpec(memory_space=pl.ANY)],
        [],
        2 * share * width * width,
        4 << 20,
        "hidden_step",
    )(parts, weight, after)


def grads_kernel(a, b, c, d, agg, pre, hidden, weight, term, out):
    grad_sum = (
        a[...].astype(F32) + b[...].astype(F32) + c[...].astype(F32) + d[...].astype(F32)
    ).astype(BF)
    grad_hidden = lax.dot_general(grad_sum, weight[...], COLS, preferred_element_type=F32)
    v = pre[...]
    gate = 1.0 / (1.0 + jnp.exp(-v))
    grad_pre = (grad_hidden * gate * (1.0 + v * (1.0 - gate))).astype(BF)
    first = lax.dot_general(agg[...], grad_pre, ROWS, preferred_element_type=F32)
    second = lax.dot_general(hidden[0], grad_sum, ROWS, preferred_element_type=F32) + term[...]
    deep, wide = out.shape[2:]
    for n, value in enumerate((first, second)):
        value = value.astype(BF)
        for i in range(out.shape[0]):
            for s in range(out.shape[1] // 2):
                out[i, n * (out.shape[1] // 2) + s] = value[
                    i * deep : (i + 1) * deep, s * wide : (s + 1) * wide
                ]


def grads_step(parts, agg, pre, hidden, weight, term):
    share, width = agg.shape
    return call(
        grads_kernel,
        jax.ShapeDtypeStruct((width // 16, 2 * width // 128, 16, 128), BF),
        [VMEM] * 9,
        [],
        6 * share * width * width,
        5 << 20,
        "grads_step",
    )(*parts, agg, pre, hidden, weight, term)


def swap_sum(x, axis):
    got = lax.all_to_all(x, axis, split_axis=0, concat_axis=0, tiled=True)
    return jnp.sum(got.astype(F32), axis=0)


def share_out(x, axis, n):
    many = jnp.broadcast_to(x[None], (n, *x.shape))
    return lax.all_to_all(many, axis, split_axis=0, concat_axis=0, tiled=True)


def hop(x, axis, n, step):
    return lax.ppermute(x, axis, [(i, (i + step) % n) for i in range(n)])


def add(*terms):
    return sum(t.astype(F32) for t in terms).astype(BF)


def shifts(parts, axis, n):
    return [parts[0]] + [hop(parts[t], axis, n, t) for t in range(1, n)]


def ring_reduce(block, z):
    half = RING // 2
    top, low = block(half)
    rows = top.shape[0]
    up = hop(top.astype(BF), "z", RING, 1)
    down = hop(low.astype(BF), "z", RING, -1)
    for s in range(half - 1, 0, -1):
        top, low = block(s)
        if s == half - 1:
            up = jnp.concatenate([top + up.astype(F32), low], axis=0).astype(BF)
            top, low = block(-s)
            down = jnp.concatenate([top, low + down.astype(F32)], axis=0).astype(BF)
        else:
            up = (jnp.concatenate([top, low], axis=0) + up.astype(F32)).astype(BF)
            down = (jnp.concatenate(block(-s), axis=0) + down.astype(F32)).astype(BF)
        up, down = hop(up, "z", RING, 1), hop(down, "z", RING, -1)
    return add(jnp.concatenate(block(0), axis=0), up, down)


def local(
    everyone,
    features,
    tile_data,
    tile_ids,
    tile_counts,
    hist_tiles,
    hist_ids,
    hist_cache,
    first_weight,
    second_weight,
    grad_out,
):
    share, width = features.shape
    scale = 1.0 / math.sqrt(share * everyone)
    core = lax.axis_index("core").astype(jnp.int32)
    z = lax.axis_index("z").astype(jnp.int32)
    y, x = (lax.axis_index(a).astype(jnp.int32) for a in ("y", "x"))
    where = jnp.stack([z, core, y, x])
    rows, panels = tile_data.shape[:2]

    numbers = jnp.concatenate([tile_ids, tile_counts[:, :, None]], axis=2)
    away = (1 - core) * (panels // 2)
    num_b = lax.ppermute(
        lax.dynamic_slice_in_dim(numbers, away, panels // 2, axis=1), "core", SWAP
    )
    tile_b = lax.ppermute(
        lax.dynamic_slice_in_dim(tile_data, away, panels // 2, axis=1), "core", SWAP
    )
    link = jnp.pad(hist_ids.T.astype(BF), ((0, 15), (0, TILE - rows)))
    link = jnp.concatenate([hist_tiles.reshape(rows * TILE, TILE), link], axis=0)

    rows_a = ring(jnp.concatenate([features, grad_out], axis=1))
    rows_b = lax.ppermute(rows_a, "core", SWAP)
    operands = where, numbers, num_b, tile_data, tile_b
    chips = SIDE * SIDE
    first = back_product(
        first_back_kernel,
        jax.ShapeDtypeStruct((chips, share, width), BF),
        *operands,
        rows_a,
        rows_b,
    )
    first, rows_a, rows_b = lax.optimization_barrier((first, rows_a, rows_b))
    first = lax.all_to_all(first, ("y", "x"), split_axis=0, concat_axis=0, tiled=True)
    quarter = jax.ShapeDtypeStruct((SIDE, share, width), BF)
    second = back_product(second_back_kernel, (quarter,) * SIDE, *operands, rows_a, rows_b)
    *second, link = lax.optimization_barrier((*second, link))
    started = second[0]
    links = shifts([link] * RING, "z", RING)
    link_ids = jnp.stack([piece[rows * TILE, :rows] for piece in links]).astype(jnp.int32)
    second = shifts(second, "x", SIDE)
    second = shifts([add(*(part[t] for part in second)) for t in range(SIDE)], "y", SIDE)
    history, hist_term = hist_product(where, link_ids, hist_cache, rows_a, links)

    first_agg, first_pre, hidden = hidden_step(first, first_weight, started)
    pair = lax.all_to_all(hidden, ("y", "x"), split_axis=0, concat_axis=0, tiled=True)
    pair = pair.reshape(chips * share, width)
    terms = grads_step(second, first_agg, first_pre, hidden, second_weight, hist_term)
    sent = partner_product(where, num_b, tile_b, pair)
    terms, sent = lax.optimization_barrier((terms, sent))
    taken = lax.ppermute(sent, "core", SWAP)
    kept = own_product(where, numbers, tile_data, pair, history)
    terms = swap_sum(terms, ROW).astype(BF)
    term = (swap_sum(terms, "z") * scale).astype(BF)
    spread = share_out(share_out(term, "z", RING).reshape(RING, 16, 128), ROW, everyone // RING)
    grads = spread.reshape(width // 16, 2 * width // 128, 16, 128).transpose(0, 2, 1, 3)
    grads = grads.reshape(width, 2 * width).astype(F32)

    def block(offset):
        at = ((z + offset) & (RING - 1)) * share
        size = share // 2
        return [
            lax.dynamic_slice_in_dim(kept, at + n * size, size)
            + lax.dynamic_slice_in_dim(taken, at + n * size, size).astype(F32)
            for n in range(2)
        ]

    second_agg = ring_reduce(block, z)
    embedding = jnp.dot(second_agg, second_weight, preferred_element_type=F32).astype(BF)
    return (embedding, grads[:, :width], grads[:, width:])


def solution(mesh):
    chip_mesh = Mesh(mesh.devices.reshape(4, 4, 2, 8), ("y", "x", "core", "z"))
    placed = (
        P(ALL, None),
        P(ROW, "z", None, None, None),
        P(ROW, "z", None),
        P(ROW, "z"),
        P(ROW, "z", None, None),
        P(ROW, "z"),
        P("z", None),
        P(),
        P(),
        P(ALL, None),
    )
    return jax.shard_map(
        functools.partial(local, 256),
        mesh=chip_mesh,
        in_specs=placed,
        out_specs=(P(ALL, None), P(), P()),
        check_vma=False,
    )
```

```python
import functools
import math

import jax
import jax.numpy as jnp
from jax import lax
from jax.experimental import pallas as pl
from jax.experimental.pallas import tpu as pltpu
from jax.sharding import Mesh, PartitionSpec as P

BF = jnp.bfloat16
F32 = jnp.float32
TILE = 128
VMEM = pl.BlockSpec(memory_space=pltpu.VMEM)
SMEM = pl.BlockSpec(memory_space=pltpu.SMEM)
ROWS = (((0,), (0,)), ((), ()))
COLS = (((1,), (1,)), ((), ()))
ROW = ("y", "x", "core")
ALL = ("y", "x", "core", "z")
SWAP = [(0, 1), (1, 0)]
RING = 8
SIDE = 4


def call(kernel, out_shape, specs, scratch, flops, moved, name):
    return pl.pallas_call(
        kernel,
        out_shape=out_shape,
        in_specs=specs,
        out_specs=jax.tree.map(lambda _: VMEM, out_shape),
        scratch_shapes=scratch,
        compiler_params=pltpu.CompilerParams(vmem_limit_bytes=40 << 20),
        cost_estimate=pl.CostEstimate(flops=flops, bytes_accessed=moved, transcendentals=0),
        name=name,
    )


def block_rows(index):
    return pl.ds(pl.multiple_of(index * TILE, TILE), TILE)


def ring_slot(source, mine):
    off = (source - mine) & (RING - 1)
    return jnp.where(off < RING // 2, 2 * off, 2 * RING - 1 - 2 * off)


def ring(x):
    up = [(i, (i + 1) % RING) for i in range(RING)]
    down = [(i, (i - 1) % RING) for i in range(RING)]
    half = x.shape[0] // 2
    pieces, u, d = [x], x, x
    for _ in range(RING // 2 - 1):
        u, d = lax.ppermute(u, "z", up), lax.ppermute(d, "z", down)
        pieces += [u, d]
    pieces += [lax.ppermute(u[:half], "z", up), lax.ppermute(d[half:], "z", down)]
    return jnp.concatenate(pieces, axis=0)


def back_sums(column, where, num_a, num_b, tile_a, tile_b, src_a, src_b, total):
    z, core = where[0], where[1]
    rows, panels, slots = tile_b.shape[:3]
    columns = total.shape[0] // panels // TILE
    lanes = pl.ds(column, total.shape[1])
    total[...] = jnp.zeros_like(total)
    for num, tiles, src, first in (
        (num_a, tile_a, src_a, panels * core),
        (num_b, tile_b, src_b, 0),
    ):

        def one_row(i, carry):
            block = src[block_rows(ring_slot(i, z)), lanes]
            parts = []
            for j in range(panels):
                used = num[i, first + j, slots]
                for t in range(slots):
                    tile = tiles[i, first + j, t]
                    tile = jnp.where(t < used, tile, jnp.zeros_like(tile))
                    part = lax.dot_general(tile, block, ROWS, preferred_element_type=F32)
                    parts.append((j * columns + num[i, first + j, t], part))
            for place, part in parts:
                total[block_rows(place), :] += part
            return carry

        lax.fori_loop(0, rows, one_row, 0, unroll=2)


def first_back_kernel(*refs):
    out, total = refs[-2:]
    back_sums(0, *refs[:-2], total)
    for a in range(out.shape[0]):
        out[a] = total[pl.ds(a * TILE, TILE), :].astype(BF)


def second_back_kernel(*refs):
    outs, total = refs[7:-1], refs[-1]
    where = refs[0]
    back_sums(total.shape[1], *refs[:7], total)
    for s in range(SIDE):
        for t in range(SIDE):
            block = ((where[2] + t) & (SIDE - 1)) * SIDE + ((where[3] + s) & (SIDE - 1))
            outs[s][t] = total[block_rows(block), :].astype(BF)


def back_product(kernel, out_shape, *operands):
    rows, panels, slots = operands[4].shape[:3]
    height, width = panels * 8 * TILE, operands[5].shape[1] // 2
    return call(
        kernel,
        out_shape,
        [SMEM] * 3 + [VMEM] * 4,
        [pltpu.VMEM((height, width), F32)],
        4 * rows * panels * slots * TILE * TILE * width,
        8 << 20,
        "back_product",
    )(*operands)


def row_blocks(where, num, tiles, source, first, start, out):
    rows, _, slots = tiles.shape[:3]
    panels = 2
    columns = source.shape[0] // panels // TILE

    def one_row(i, carry):
        at = block_rows(i)
        acc = start[at, :] if start is not None else jnp.zeros((TILE, out.shape[1]), F32)
        for j in range(panels):
            used = num[i, first + j, slots]
            for t in range(slots):
                tile = tiles[i, first + j, t]
                tile = jnp.where(t < used, tile, jnp.zeros_like(tile))
                part = source[block_rows(j * columns + num[i, first + j, t]), :]
                acc += jnp.dot(tile, part, preferred_element_type=F32)
        out[at, :] = acc.astype(out.dtype)
        return carry

    lax.fori_loop(0, rows, one_row, 0, unroll=2)


def partner_kernel(where, num, tiles, pair, *refs):
    row_blocks(where, num, tiles, pair, 0, None, refs[-1])


def own_kernel(where, num, tiles, pair, history, out):
    row_blocks(where, num, tiles, pair, 2 * where[1], history, out)


def partner_product(where, num, tiles, pair, *after):
    rows, width = tiles.shape[0], pair.shape[1]
    return call(
        partner_kernel,
        jax.ShapeDtypeStruct((rows * TILE, width), BF),
        [SMEM] * 2 + [VMEM] * 2 + [pl.BlockSpec(memory_space=pl.ANY)] * len(after),
        [],
        8 * rows * TILE * TILE * width,
        4 << 20,
        "row_product",
    )(where, num, tiles, pair, *after)


def own_product(where, num, tiles, pair, history):
    rows, width = tiles.shape[0], pair.shape[1]
    return call(
        own_kernel,
        jax.ShapeDtypeStruct((rows * TILE, width), F32),
        [SMEM] * 2 + [VMEM] * 3,
        [],
        8 * rows * TILE * TILE * width,
        5 << 20,
        "row_product",
    )(where, num, tiles, pair, history)


def hist_kernel(where, ids, cache, grads, *refs):
    pieces, (out, term, held, sems) = refs[:-4], refs[-4:]
    copies = [
        pltpu.make_async_copy(piece, held.at[n], sems.at[n]) for n, piece in enumerate(pieces)
    ]
    for copy in copies:
        copy.start()
    blocks = cache.shape[0] // TILE
    z = where[0]
    rows = ids.shape[1]
    out[...] = jnp.zeros_like(out)
    for n, copy in enumerate(copies):
        copy.wait()

        def one_row(p, carry):
            block = ids[n, p] - z * blocks

            @pl.when((block >= 0) & (block < blocks))
            def _():
                out[block_rows(p), :] += jnp.dot(
                    held[n, block_rows(p), :],
                    cache[block_rows(block), :],
                    preferred_element_type=F32,
                )

            return carry

        lax.fori_loop(0, rows, one_row, 0)
    term[...] = jnp.zeros_like(term)

    def one_term(p, carry):
        term[...] += lax.dot_general(
            out[block_rows(p), :].astype(BF),
            grads[block_rows(ring_slot(p, z)), pl.ds(term.shape[1], term.shape[1])],
            ROWS,
            preferred_element_type=F32,
        )
        return carry

    lax.fori_loop(0, rows, one_term, 0)


def hist_product(where, ids, cache, grads, pieces):
    rows, width = ids.shape[1], cache.shape[1]
    return call(
        hist_kernel,
        (
            jax.ShapeDtypeStruct((rows * TILE, width), F32),
            jax.ShapeDtypeStruct((width, width), F32),
        ),
        [SMEM] * 2 + [VMEM] * 2 + [pl.BlockSpec(memory_space=pl.ANY)] * len(pieces),
        [
            pltpu.VMEM((len(pieces), *pieces[0].shape), BF),
            pltpu.SemaphoreType.DMA((len(pieces),)),
        ],
        2 * rows * TILE * TILE * width + 2 * rows * TILE * width * width,
        6 << 20,
        "hist_product",
    )(where, ids, cache, grads, *pieces)


def hidden_kernel(parts, weight, *refs):
    agg, pre, hidden = refs[-3:]
    total = parts[0].astype(F32)
    for i in range(1, parts.shape[0]):
        total += parts[i].astype(F32)
    agg[...] = total.astype(BF)
    v = jnp.dot(agg[...], weight[...], preferred_element_type=F32)
    pre[...] = v
    h = (v * (1.0 / (1.0 + jnp.exp(-v)))).astype(BF)
    for i in range(hidden.shape[0]):
        hidden[i] = h


def hidden_step(parts, weight, *after):
    share, width = parts.shape[1:]
    return call(
        hidden_kernel,
        (
            jax.ShapeDtypeStruct((share, width), BF),
            jax.ShapeDtypeStruct((share, width), F32),
            jax.ShapeDtypeStruct(parts.shape, BF),
        ),
        [VMEM] * 2 + [pl.BlockSpec(memory_space=pl.ANY)] * len(after),
        [],
        2 * share * width * width,
        4 << 20,
        "hidden_step",
    )(parts, weight, *after)


def grads_kernel(a, b, c, d, agg, pre, hidden, weight, term, after, out):
    grad_sum = (
        a[...].astype(F32) + b[...].astype(F32) + c[...].astype(F32) + d[...].astype(F32)
    ).astype(BF)
    grad_hidden = lax.dot_general(grad_sum, weight[...], COLS, preferred_element_type=F32)
    v = pre[...]
    gate = 1.0 / (1.0 + jnp.exp(-v))
    grad_pre = (grad_hidden * gate * (1.0 + v * (1.0 - gate))).astype(BF)
    first = lax.dot_general(agg[...], grad_pre, ROWS, preferred_element_type=F32)
    second = lax.dot_general(hidden[0], grad_sum, ROWS, preferred_element_type=F32) + term[...]
    deep, wide = out.shape[2:]
    for n, value in enumerate((first, second)):
        value = value.astype(BF)
        for i in range(out.shape[0]):
            for s in range(out.shape[1] // 2):
                out[i, n * (out.shape[1] // 2) + s] = value[
                    i * deep : (i + 1) * deep, s * wide : (s + 1) * wide
                ]


def grads_step(parts, agg, pre, hidden, weight, term, after):
    share, width = agg.shape
    return call(
        grads_kernel,
        jax.ShapeDtypeStruct((width // 16, 2 * width // 128, 16, 128), BF),
        [VMEM] * 9 + [pl.BlockSpec(memory_space=pl.ANY)],
        [],
        6 * share * width * width,
        5 << 20,
        "grads_step",
    )(*parts, agg, pre, hidden, weight, term, after)


def swap_sum(x, axis):
    got = lax.all_to_all(x, axis, split_axis=0, concat_axis=0, tiled=True)
    return jnp.sum(got.astype(F32), axis=0)


def share_out(x, axis, n):
    many = jnp.broadcast_to(x[None], (n, *x.shape))
    return lax.all_to_all(many, axis, split_axis=0, concat_axis=0, tiled=True)


def hop(x, axis, n, step):
    return lax.ppermute(x, axis, [(i, (i + step) % n) for i in range(n)])


def add(*terms):
    return sum(t.astype(F32) for t in terms).astype(BF)


def shifts(parts, axis, n):
    return [parts[0]] + [hop(parts[t], axis, n, t) for t in range(1, n)]


def ring_reduce(block, z):
    half = RING // 2
    top, low = block(half)
    rows = top.shape[0]
    up = hop(top.astype(BF), "z", RING, 1)
    down = hop(low.astype(BF), "z", RING, -1)
    for s in range(half - 1, 0, -1):
        top, low = block(s)
        if s == half - 1:
            up = jnp.concatenate([top + up.astype(F32), low], axis=0).astype(BF)
            top, low = block(-s)
            down = jnp.concatenate([top, low + down.astype(F32)], axis=0).astype(BF)
        else:
            up = (jnp.concatenate([top, low], axis=0) + up.astype(F32)).astype(BF)
            down = (jnp.concatenate(block(-s), axis=0) + down.astype(F32)).astype(BF)
        up, down = hop(up, "z", RING, 1), hop(down, "z", RING, -1)
    return add(jnp.concatenate(block(0), axis=0), up, down)


def local(
    everyone,
    features,
    tile_data,
    tile_ids,
    tile_counts,
    hist_tiles,
    hist_ids,
    hist_cache,
    first_weight,
    second_weight,
    grad_out,
):
    share, width = features.shape
    scale = 1.0 / math.sqrt(share * everyone)
    core = lax.axis_index("core").astype(jnp.int32)
    z = lax.axis_index("z").astype(jnp.int32)
    y, x = (lax.axis_index(a).astype(jnp.int32) for a in ("y", "x"))
    where = jnp.stack([z, core, y, x])
    rows, panels = tile_data.shape[:2]

    numbers = jnp.concatenate([tile_ids, tile_counts[:, :, None]], axis=2)
    away = (1 - core) * (panels // 2)
    num_b = lax.ppermute(
        lax.dynamic_slice_in_dim(numbers, away, panels // 2, axis=1), "core", SWAP
    )
    tile_b = lax.ppermute(
        lax.dynamic_slice_in_dim(tile_data, away, panels // 2, axis=1), "core", SWAP
    )
    link = jnp.pad(hist_ids.T.astype(BF), ((0, 15), (0, TILE - rows)))
    link = jnp.concatenate([hist_tiles.reshape(rows * TILE, TILE), link], axis=0)

    rows_a = ring(jnp.concatenate([features, grad_out], axis=1))
    rows_b = lax.ppermute(rows_a, "core", SWAP)
    operands = where, numbers, num_b, tile_data, tile_b
    chips = SIDE * SIDE
    first = back_product(
        first_back_kernel,
        jax.ShapeDtypeStruct((chips, share, width), BF),
        *operands,
        rows_a,
        rows_b,
    )
    first, rows_a, rows_b = lax.optimization_barrier((first, rows_a, rows_b))
    first = lax.all_to_all(first, ("y", "x"), split_axis=0, concat_axis=0, tiled=True)
    quarter = jax.ShapeDtypeStruct((SIDE, share, width), BF)
    second = back_product(second_back_kernel, (quarter,) * SIDE, *operands, rows_a, rows_b)
    *second, link = lax.optimization_barrier((*second, link))
    links = shifts([link] * RING, "z", RING)
    link_ids = jnp.stack([piece[rows * TILE, :rows] for piece in links]).astype(jnp.int32)
    second = shifts(second, "x", SIDE)
    blocks = [add(*(part[t] for part in second)) for t in range(SIDE)]
    second = shifts(blocks, "y", SIDE)
    history, hist_term = hist_product(where, link_ids, hist_cache, rows_a, links)

    first_agg, first_pre, hidden = hidden_step(
        first, first_weight, blocks[1], *links[1:3], *links[6:]
    )
    pair = lax.all_to_all(hidden, ("y", "x"), split_axis=0, concat_axis=0, tiled=True)
    pair = pair.reshape(chips * share, width)
    sent = partner_product(where, num_b, tile_b, pair, hist_term, *second[1:])
    taken = lax.ppermute(sent, "core", SWAP)
    terms = grads_step(second, first_agg, first_pre, hidden, second_weight, hist_term, sent)
    terms = swap_sum(terms, ROW).astype(BF)
    term = lax.all_to_all(jnp.broadcast_to(terms[None], (RING, *terms.shape)), "z", 0, 0)
    term = (jnp.sum(term.astype(F32), axis=0) * scale).astype(BF)
    spread = share_out(term, ROW, everyone // RING)
    grads = spread.reshape(width // 16, 2 * width // 128, 16, 128).transpose(0, 2, 1, 3)
    grads = grads.reshape(width, 2 * width).astype(F32)
    kept = own_product(where, numbers, tile_data, pair, history)

    def block(offset):
        at = ((z + offset) & (RING - 1)) * share
        size = share // 2
        return [
            lax.dynamic_slice_in_dim(kept, at + n * size, size)
            + lax.dynamic_slice_in_dim(taken, at + n * size, size).astype(F32)
            for n in range(2)
        ]

    second_agg = ring_reduce(block, z)
    embedding = jnp.dot(second_agg, second_weight, preferred_element_type=F32).astype(BF)
    return (embedding, grads[:, :width], grads[:, width:])


def solution(mesh):
    chip_mesh = Mesh(mesh.devices.reshape(4, 4, 2, 8), ("y", "x", "core", "z"))
    placed = (
        P(ALL, None),
        P(ROW, "z", None, None, None),
        P(ROW, "z", None),
        P(ROW, "z"),
        P(ROW, "z", None, None),
        P(ROW, "z"),
        P("z", None),
        P(),
        P(),
        P(ALL, None),
    )
    return jax.shard_map(
        functools.partial(local, 256),
        mesh=chip_mesh,
        in_specs=placed,
        out_specs=(P(ALL, None), P(), P()),
        check_vma=False,
    )
```

```python
import functools
import math

import jax
import jax.numpy as jnp
from jax import lax
from jax.experimental import pallas as pl
from jax.experimental.pallas import tpu as pltpu
from jax.sharding import Mesh, PartitionSpec as P

BF = jnp.bfloat16
F32 = jnp.float32
TILE = 128
VMEM = pl.BlockSpec(memory_space=pltpu.VMEM)
SMEM = pl.BlockSpec(memory_space=pltpu.SMEM)
ROWS = (((0,), (0,)), ((), ()))
COLS = (((1,), (1,)), ((), ()))
ROW = ("y", "x", "core")
ALL = ("y", "x", "core", "z")
SWAP = [(0, 1), (1, 0)]
RING = 8
SIDE = 4


def call(kernel, out_shape, specs, scratch, flops, moved, name, room=40):
    return pl.pallas_call(
        kernel,
        out_shape=out_shape,
        in_specs=specs,
        out_specs=jax.tree.map(lambda _: VMEM, out_shape),
        scratch_shapes=scratch,
        compiler_params=pltpu.CompilerParams(vmem_limit_bytes=room << 20),
        cost_estimate=pl.CostEstimate(flops=flops, bytes_accessed=moved, transcendentals=0),
        name=name,
    )


def block_rows(index):
    return pl.ds(pl.multiple_of(index * TILE, TILE), TILE)


def ring_slot(source, mine):
    off = (source - mine) & (RING - 1)
    return jnp.where(off < RING // 2, 2 * off, 2 * RING - 1 - 2 * off)


def ring(x):
    up = [(i, (i + 1) % RING) for i in range(RING)]
    down = [(i, (i - 1) % RING) for i in range(RING)]
    half = x.shape[0] // 2
    pieces, u, d = [x], x, x
    for _ in range(RING // 2 - 1):
        u, d = lax.ppermute(u, "z", up), lax.ppermute(d, "z", down)
        pieces += [u, d]
    pieces += [lax.ppermute(u[:half], "z", up), lax.ppermute(d[half:], "z", down)]
    return jnp.concatenate(pieces, axis=0)


def back_sums(column, where, num_a, num_b, tile_a, tile_b, src_a, src_b, total):
    z, core = where[0], where[1]
    rows, panels, slots = tile_b.shape[:3]
    columns = total.shape[0] // panels // TILE
    lanes = pl.ds(column, total.shape[1])
    total[...] = jnp.zeros_like(total)
    for num, tiles, src, first in (
        (num_a, tile_a, src_a, panels * core),
        (num_b, tile_b, src_b, 0),
    ):

        def one_row(i, carry):
            block = src[block_rows(ring_slot(i, z)), lanes]
            parts = []
            for j in range(panels):
                used = num[i, first + j, slots]
                for t in range(slots):
                    tile = tiles[i, first + j, t]
                    tile = jnp.where(t < used, tile, jnp.zeros_like(tile))
                    part = lax.dot_general(tile, block, ROWS, preferred_element_type=F32)
                    parts.append((j * columns + num[i, first + j, t], part))
            for place, part in parts:
                total[block_rows(place), :] += part
            return carry

        lax.fori_loop(0, rows, one_row, 0, unroll=2)


def first_back_kernel(*refs):
    out, total = refs[-2:]
    back_sums(0, *refs[:-2], total)
    for a in range(out.shape[0]):
        out[a] = total[pl.ds(a * TILE, TILE), :].astype(BF)


def second_back_kernel(*refs):
    outs, total = refs[7:-1], refs[-1]
    where = refs[0]
    back_sums(total.shape[1], *refs[:7], total)
    for s in range(SIDE):
        for t in range(SIDE):
            block = ((where[2] + t) & (SIDE - 1)) * SIDE + ((where[3] + s) & (SIDE - 1))
            value = total[block_rows(block), :].astype(BF)
            if s == 2:
                outs[2 + t // 2][t % 2] = value
            else:
                outs[(0, 1, None, 4)[s]][t] = value


def back_product(kernel, out_shape, *operands):
    rows, panels, slots = operands[4].shape[:3]
    height, width = panels * 8 * TILE, operands[5].shape[1] // 2
    return call(
        kernel,
        out_shape,
        [SMEM] * 3 + [VMEM] * 4,
        [pltpu.VMEM((height, width), F32)],
        4 * rows * panels * slots * TILE * TILE * width,
        8 << 20,
        "back_product",
    )(*operands)


def row_blocks(where, num, tiles, source, first, start, out):
    rows, _, slots = tiles.shape[:3]
    panels = 2
    columns = source.shape[0] // panels // TILE

    def one_row(i, carry):
        at = block_rows(i)
        acc = start[at, :] if start is not None else jnp.zeros((TILE, out.shape[1]), F32)
        for j in range(panels):
            used = num[i, first + j, slots]
            for t in range(slots):
                tile = tiles[i, first + j, t]
                tile = jnp.where(t < used, tile, jnp.zeros_like(tile))
                part = source[block_rows(j * columns + num[i, first + j, t]), :]
                acc += jnp.dot(tile, part, preferred_element_type=F32)
        out[at, :] = acc.astype(out.dtype)
        return carry

    lax.fori_loop(0, rows, one_row, 0, unroll=2)


def partner_kernel(where, num, tiles, pair, out):
    row_blocks(where, num, tiles, pair, 0, None, out)


def own_kernel(where, num, tiles, pair, history, out):
    row_blocks(where, num, tiles, pair, 2 * where[1], history, out)


def partner_product(where, num, tiles, pair):
    rows, width = tiles.shape[0], pair.shape[1]
    return call(
        partner_kernel,
        jax.ShapeDtypeStruct((rows * TILE, width), BF),
        [SMEM] * 2 + [VMEM] * 2,
        [],
        8 * rows * TILE * TILE * width,
        4 << 20,
        "row_product",
    )(where, num, tiles, pair)


def own_product(where, num, tiles, pair, history):
    rows, width = tiles.shape[0], pair.shape[1]
    return call(
        own_kernel,
        jax.ShapeDtypeStruct((rows * TILE, width), F32),
        [SMEM] * 2 + [VMEM] * 3,
        [],
        8 * rows * TILE * TILE * width,
        5 << 20,
        "row_product",
    )(where, num, tiles, pair, history)


def hist_kernel(where, ids, cache, grads, *refs):
    pieces, (out, term, held, sems) = refs[:-4], refs[-4:]
    copies = [
        pltpu.make_async_copy(piece, held.at[n], sems.at[n]) for n, piece in enumerate(pieces)
    ]
    for copy in copies:
        copy.start()
    blocks = cache.shape[0] // TILE
    z = where[0]
    rows = ids.shape[1]
    out[...] = jnp.zeros_like(out)
    for n, copy in enumerate(copies):
        copy.wait()

        def one_row(p, carry):
            block = ids[n, p] - z * blocks

            @pl.when((block >= 0) & (block < blocks))
            def _():
                out[block_rows(p), :] += jnp.dot(
                    held[n, block_rows(p), :],
                    cache[block_rows(block), :],
                    preferred_element_type=F32,
                )

            return carry

        lax.fori_loop(0, rows, one_row, 0)
    term[...] = jnp.zeros_like(term)

    def one_term(p, carry):
        term[...] += lax.dot_general(
            out[block_rows(p), :].astype(BF),
            grads[block_rows(ring_slot(p, z)), pl.ds(term.shape[1], term.shape[1])],
            ROWS,
            preferred_element_type=F32,
        )
        return carry

    lax.fori_loop(0, rows, one_term, 0)


def hist_product(where, ids, cache, grads, pieces):
    rows, width = ids.shape[1], cache.shape[1]
    return call(
        hist_kernel,
        (
            jax.ShapeDtypeStruct((rows * TILE, width), F32),
            jax.ShapeDtypeStruct((width, width), F32),
        ),
        [SMEM] * 2 + [VMEM] * 2 + [pl.BlockSpec(memory_space=pl.ANY)] * len(pieces),
        [
            pltpu.VMEM((len(pieces), *pieces[0].shape), BF),
            pltpu.SemaphoreType.DMA((len(pieces),)),
        ],
        2 * rows * TILE * TILE * width + 2 * rows * TILE * width * width,
        6 << 20,
        "hist_product",
        58,
    )(where, ids, cache, grads, *pieces)


def hidden_kernel(parts, weight, agg, pre, hidden):
    total = parts[0].astype(F32)
    for i in range(1, parts.shape[0]):
        total += parts[i].astype(F32)
    agg[...] = total.astype(BF)
    v = jnp.dot(agg[...], weight[...], preferred_element_type=F32)
    pre[...] = v
    h = (v * (1.0 / (1.0 + jnp.exp(-v)))).astype(BF)
    for i in range(hidden.shape[0]):
        hidden[i] = h


def hidden_step(parts, weight):
    share, width = parts.shape[1:]
    return call(
        hidden_kernel,
        (
            jax.ShapeDtypeStruct((share, width), BF),
            jax.ShapeDtypeStruct((share, width), F32),
            jax.ShapeDtypeStruct(parts.shape, BF),
        ),
        [VMEM] * 2,
        [],
        2 * share * width * width,
        4 << 20,
        "hidden_step",
    )(parts, weight)


def grads_kernel(a, b, c, d, agg, pre, hidden, weight, term, out):
    grad_sum = (
        a[...].astype(F32) + b[...].astype(F32) + c[...].astype(F32) + d[...].astype(F32)
    ).astype(BF)
    grad_hidden = lax.dot_general(grad_sum, weight[...], COLS, preferred_element_type=F32)
    v = pre[...]
    gate = 1.0 / (1.0 + jnp.exp(-v))
    grad_pre = (grad_hidden * gate * (1.0 + v * (1.0 - gate))).astype(BF)
    first = lax.dot_general(agg[...], grad_pre, ROWS, preferred_element_type=F32)
    second = lax.dot_general(hidden[0], grad_sum, ROWS, preferred_element_type=F32) + term[...]
    deep, wide = out.shape[2:]
    for n, value in enumerate((first, second)):
        value = value.astype(BF)
        for i in range(out.shape[0]):
            for s in range(out.shape[1] // 2):
                out[i, n * (out.shape[1] // 2) + s] = value[
                    i * deep : (i + 1) * deep, s * wide : (s + 1) * wide
                ]


def grads_step(parts, agg, pre, hidden, weight, term):
    share, width = agg.shape
    return call(
        grads_kernel,
        jax.ShapeDtypeStruct((width // 16, 2 * width // 128, 16, 128), BF),
        [VMEM] * 9,
        [],
        6 * share * width * width,
        5 << 20,
        "grads_step",
    )(*parts, agg, pre, hidden, weight, term)


def swap_sum(x, axis):
    got = lax.all_to_all(x, axis, split_axis=0, concat_axis=0, tiled=True)
    return jnp.sum(got.astype(F32), axis=0)


def share_out(x, axis, n):
    many = jnp.broadcast_to(x[None], (n, *x.shape))
    return lax.all_to_all(many, axis, split_axis=0, concat_axis=0, tiled=True)


def hop(x, axis, n, step):
    return lax.ppermute(x, axis, [(i, (i + step) % n) for i in range(n)])


def after(x, *others):
    return lax.optimization_barrier((x, *others))[0]


def add(*terms):
    return sum(t.astype(F32) for t in terms).astype(BF)


def shifts(parts, axis, n):
    return [parts[0]] + [hop(parts[t], axis, n, t) for t in range(1, n)]


def ring_reduce(block, z):
    half = RING // 2
    top, low = block(half)
    rows = top.shape[0]
    up = hop(top.astype(BF), "z", RING, 1)
    down = hop(low.astype(BF), "z", RING, -1)
    for s in range(half - 1, 0, -1):
        top, low = block(s)
        if s == half - 1:
            up = jnp.concatenate([top + up.astype(F32), low], axis=0).astype(BF)
            top, low = block(-s)
            down = jnp.concatenate([top, low + down.astype(F32)], axis=0).astype(BF)
        else:
            up = (jnp.concatenate([top, low], axis=0) + up.astype(F32)).astype(BF)
            down = (jnp.concatenate(block(-s), axis=0) + down.astype(F32)).astype(BF)
        up, down = hop(up, "z", RING, 1), hop(down, "z", RING, -1)
    return add(jnp.concatenate(block(0), axis=0), up, down)


def local(
    everyone,
    features,
    tile_data,
    tile_ids,
    tile_counts,
    hist_tiles,
    hist_ids,
    hist_cache,
    first_weight,
    second_weight,
    grad_out,
):
    share, width = features.shape
    scale = 1.0 / math.sqrt(share * everyone)
    core = lax.axis_index("core").astype(jnp.int32)
    z = lax.axis_index("z").astype(jnp.int32)
    y, x = (lax.axis_index(a).astype(jnp.int32) for a in ("y", "x"))
    where = jnp.stack([z, core, y, x])
    rows, panels = tile_data.shape[:2]

    numbers = jnp.concatenate([tile_ids, tile_counts[:, :, None]], axis=2)
    away = (1 - core) * (panels // 2)
    num_b = lax.ppermute(
        lax.dynamic_slice_in_dim(numbers, away, panels // 2, axis=1), "core", SWAP
    )
    tile_b = lax.ppermute(
        lax.dynamic_slice_in_dim(tile_data, away, panels // 2, axis=1), "core", SWAP
    )
    link = jnp.pad(hist_ids.T.astype(BF), ((0, 15), (0, TILE - rows)))
    link = jnp.concatenate([hist_tiles.reshape(rows * TILE, TILE), link], axis=0)

    rows_a = ring(jnp.concatenate([features, grad_out], axis=1))
    rows_b = lax.ppermute(rows_a, "core", SWAP)
    operands = where, numbers, num_b, tile_data, tile_b
    chips = SIDE * SIDE
    first = back_product(
        first_back_kernel,
        jax.ShapeDtypeStruct((chips, share, width), BF),
        *operands,
        rows_a,
        rows_b,
    )
    first, rows_a, rows_b = lax.optimization_barrier((first, rows_a, rows_b))
    first = lax.all_to_all(first, ("y", "x"), split_axis=0, concat_axis=0, tiled=True)
    shapes = tuple(jax.ShapeDtypeStruct((n, share, width), BF) for n in (4, 4, 2, 2, 4))
    second = back_product(second_back_kernel, shapes, *operands, rows_a, rows_b)
    *second, link = lax.optimization_barrier((*second, link))
    links = shifts([link] * RING, "z", RING)
    link_ids = jnp.stack([piece[rows * TILE, :rows] for piece in links]).astype(jnp.int32)
    own, near, far_up, far_down, back = second
    up, down = hop(far_up, "x", SIDE, 1), hop(far_down, "x", SIDE, -1)
    near = jnp.concatenate([add(near[:2], up), near[2:]], axis=0)
    back = jnp.concatenate([back[:2], add(back[2:], down)], axis=0)
    up, down = hop(near, "x", SIDE, 1), hop(back, "x", SIDE, -1)
    blocks = [add(own[t], up[t], down[t]) for t in range(SIDE)]
    second = shifts(blocks, "y", SIDE)
    history, hist_term = hist_product(where, link_ids, hist_cache, rows_a, links)

    first_agg, first_pre, hidden = hidden_step(after(first, *blocks, *links[1:3], *links[6:]), first_weight)
    pair = lax.all_to_all(hidden, ("y", "x"), split_axis=0, concat_axis=0, tiled=True)
    pair = pair.reshape(chips * share, width)
    pair = after(pair, hist_term, *second[1:])
    sent = partner_product(where, num_b, tile_b, pair)
    taken = lax.ppermute(sent, "core", SWAP)
    second[0] = after(second[0], pair)
    terms = grads_step(second, first_agg, first_pre, hidden, second_weight, hist_term)
    terms = swap_sum(terms, ROW).astype(BF)
    term = lax.all_to_all(jnp.broadcast_to(terms[None], (RING, *terms.shape)), "z", 0, 0)
    term = (jnp.sum(term.astype(F32), axis=0) * scale).astype(BF)
    spread = share_out(term, ROW, everyone // RING)
    grads = spread.reshape(width // 16, 2 * width // 128, 16, 128).transpose(0, 2, 1, 3)
    grads = grads.reshape(width, 2 * width).astype(F32)
    kept = own_product(where, numbers, tile_data, pair, history)

    def block(offset):
        at = ((z + offset) & (RING - 1)) * share
        size = share // 2
        return [
            lax.dynamic_slice_in_dim(kept, at + n * size, size)
            + lax.dynamic_slice_in_dim(taken, at + n * size, size).astype(F32)
            for n in range(2)
        ]

    second_agg = ring_reduce(block, z)
    embedding = jnp.dot(second_agg, second_weight, preferred_element_type=F32).astype(BF)
    return (embedding, grads[:, :width], grads[:, width:])


def solution(mesh):
    chip_mesh = Mesh(mesh.devices.reshape(4, 4, 2, 8), ("y", "x", "core", "z"))
    placed = (
        P(ALL, None),
        P(ROW, "z", None, None, None),
        P(ROW, "z", None),
        P(ROW, "z"),
        P(ROW, "z", None, None),
        P(ROW, "z"),
        P("z", None),
        P(),
        P(),
        P(ALL, None),
    )
    return jax.shard_map(
        functools.partial(local, 256),
        mesh=chip_mesh,
        in_specs=placed,
        out_specs=(P(ALL, None), P(), P()),
        check_vma=False,
    )
```

```python
import functools
import math

import jax
import jax.numpy as jnp
from jax import lax
from jax.experimental import pallas as pl
from jax.experimental.pallas import tpu as pltpu
from jax.sharding import Mesh, PartitionSpec as P

BF = jnp.bfloat16
F32 = jnp.float32
TILE = 128
VMEM = pl.BlockSpec(memory_space=pltpu.VMEM)
SMEM = pl.BlockSpec(memory_space=pltpu.SMEM)
ROWS = (((0,), (0,)), ((), ()))
COLS = (((1,), (1,)), ((), ()))
ROW = ("y", "x", "core")
ALL = ("y", "x", "core", "z")
SWAP = [(0, 1), (1, 0)]
RING = 8
SIDE = 4


def call(kernel, out_shape, specs, scratch, flops, moved, name, room=40):
    return pl.pallas_call(
        kernel,
        out_shape=out_shape,
        in_specs=specs,
        out_specs=jax.tree.map(lambda _: VMEM, out_shape),
        scratch_shapes=scratch,
        compiler_params=pltpu.CompilerParams(vmem_limit_bytes=room << 20),
        cost_estimate=pl.CostEstimate(flops=flops, bytes_accessed=moved, transcendentals=0),
        name=name,
    )


def block_rows(index):
    return pl.ds(pl.multiple_of(index * TILE, TILE), TILE)


def ring_slot(source, mine):
    off = (source - mine) & (RING - 1)
    return jnp.where(off < RING // 2, 2 * off, 2 * RING - 1 - 2 * off)


def ring(x):
    up = [(i, (i + 1) % RING) for i in range(RING)]
    down = [(i, (i - 1) % RING) for i in range(RING)]
    half = x.shape[0] // 2
    pieces, u, d = [x], x, x
    for _ in range(RING // 2 - 1):
        u, d = lax.ppermute(u, "z", up), lax.ppermute(d, "z", down)
        pieces += [u, d]
    pieces += [lax.ppermute(u[:half], "z", up), lax.ppermute(d[half:], "z", down)]
    return jnp.concatenate(pieces, axis=0)


def back_sums(where, num_a, num_b, tile_a, tile_b, src_a, src_b, total):
    z, core = where[0], where[1]
    rows, panels, slots = tile_b.shape[:3]
    columns = total.shape[0] // panels // TILE
    total[...] = jnp.zeros_like(total)
    for num, tiles, src, first in (
        (num_a, tile_a, src_a, panels * core),
        (num_b, tile_b, src_b, 0),
    ):

        def one_row(i, carry):
            block = src[block_rows(ring_slot(i, z)), :]
            parts = []
            for j in range(panels):
                used = num[i, first + j, slots]
                for t in range(slots):
                    tile = tiles[i, first + j, t]
                    tile = jnp.where(t < used, tile, jnp.zeros_like(tile))
                    part = lax.dot_general(tile, block, ROWS, preferred_element_type=F32)
                    parts.append((j * columns + num[i, first + j, t], part))
            for place, part in parts:
                total[block_rows(place), :] += part
            return carry

        lax.fori_loop(0, rows, one_row, 0, unroll=2)


def first_back_kernel(*refs):
    out, total = refs[-2:]
    back_sums(*refs[:-2], total)
    for a in range(out.shape[0]):
        out[a] = total[pl.ds(a * TILE, TILE), :].astype(BF)


def second_back_kernel(*refs):
    weight, out, turned, total = refs[7:]
    back_sums(*refs[:7], total)

    def one_chunk(i, carry):
        at = pl.ds(pl.multiple_of(i * 4 * TILE, TILE), 4 * TILE)
        value = total[at, :].astype(BF)
        out[at, :] = value
        part = lax.dot_general(value, weight[...], COLS, preferred_element_type=F32)
        turned[at, :] = part.astype(BF)
        return carry

    lax.fori_loop(0, total.shape[0] // (4 * TILE), one_chunk, 0)


def back_product(kernel, out_shape, *operands):
    rows, panels, slots = operands[4].shape[:3]
    height, width = panels * 8 * TILE, operands[5].shape[1]
    return call(
        kernel,
        out_shape,
        [SMEM] * 3 + [VMEM] * (len(operands) - 3),
        [pltpu.VMEM((height, width), F32)],
        4 * rows * panels * slots * TILE * TILE * width,
        8 << 20,
        "back_product",
    )(*operands)


def row_blocks(where, num, tiles, source, first, start, out):
    rows, _, slots = tiles.shape[:3]
    panels = 2
    columns = source.shape[0] // panels // TILE

    def one_row(i, carry):
        at = block_rows(i)
        acc = start[at, :] if start is not None else jnp.zeros((TILE, out.shape[1]), F32)
        for j in range(panels):
            used = num[i, first + j, slots]
            for t in range(slots):
                tile = tiles[i, first + j, t]
                tile = jnp.where(t < used, tile, jnp.zeros_like(tile))
                part = source[block_rows(j * columns + num[i, first + j, t]), :]
                acc += jnp.dot(tile, part, preferred_element_type=F32)
        out[at, :] = acc.astype(out.dtype)
        return carry

    lax.fori_loop(0, rows, one_row, 0, unroll=2)


def partner_kernel(where, num, tiles, pair, out):
    row_blocks(where, num, tiles, pair, 0, None, out)


def own_kernel(where, num, tiles, pair, history, out):
    row_blocks(where, num, tiles, pair, 2 * where[1], history, out)


def partner_product(where, num, tiles, pair):
    rows, width = tiles.shape[0], pair.shape[1]
    return call(
        partner_kernel,
        jax.ShapeDtypeStruct((rows * TILE, width), BF),
        [SMEM] * 2 + [VMEM] * 2,
        [],
        8 * rows * TILE * TILE * width,
        4 << 20,
        "row_product",
    )(where, num, tiles, pair)


def own_product(where, num, tiles, pair, history):
    rows, width = tiles.shape[0], pair.shape[1]
    return call(
        own_kernel,
        jax.ShapeDtypeStruct((rows * TILE, width), F32),
        [SMEM] * 2 + [VMEM] * 3,
        [],
        8 * rows * TILE * TILE * width,
        5 << 20,
        "row_product",
    )(where, num, tiles, pair, history)


def hist_kernel(where, ids, cache, grads, *refs):
    pieces, (out, term, held, sems) = refs[:-4], refs[-4:]
    copies = [
        pltpu.make_async_copy(piece, held.at[n], sems.at[n]) for n, piece in enumerate(pieces)
    ]
    for copy in copies:
        copy.start()
    blocks = cache.shape[0] // TILE
    z = where[0]
    rows = ids.shape[1]
    out[...] = jnp.zeros_like(out)
    for n, copy in enumerate(copies):
        copy.wait()

        def one_row(p, carry):
            block = ids[n, p] - z * blocks

            @pl.when((block >= 0) & (block < blocks))
            def _():
                out[block_rows(p), :] += jnp.dot(
                    held[n, block_rows(p), :],
                    cache[block_rows(block), :],
                    preferred_element_type=F32,
                )

            return carry

        lax.fori_loop(0, rows, one_row, 0)
    term[...] = jnp.zeros_like(term)

    def one_term(p, carry):
        term[...] += lax.dot_general(
            out[block_rows(p), :].astype(BF),
            grads[block_rows(ring_slot(p, z)), :],
            ROWS,
            preferred_element_type=F32,
        )
        return carry

    lax.fori_loop(0, rows, one_term, 0)


def hist_product(where, ids, cache, grads, pieces):
    rows, width = ids.shape[1], cache.shape[1]
    return call(
        hist_kernel,
        (
            jax.ShapeDtypeStruct((rows * TILE, width), F32),
            jax.ShapeDtypeStruct((width, width), F32),
        ),
        [SMEM] * 2 + [VMEM] * 2 + [pl.BlockSpec(memory_space=pl.ANY)] * len(pieces),
        [
            pltpu.VMEM((len(pieces), *pieces[0].shape), BF),
            pltpu.SemaphoreType.DMA((len(pieces),)),
        ],
        2 * rows * TILE * TILE * width + 2 * rows * TILE * width * width,
        6 << 20,
        "hist_product",
        58,
    )(where, ids, cache, grads, *pieces)


def agg_kernel(parts, out):
    total = parts[0].astype(F32)
    for i in range(1, parts.shape[0]):
        total += parts[i].astype(F32)
    total = total.astype(BF)
    for i in range(out.shape[0]):
        out[i] = total


def agg_step(parts):
    return call(
        agg_kernel,
        jax.ShapeDtypeStruct(parts.shape, BF),
        [VMEM],
        [],
        parts.size,
        4 << 20,
        "agg_step",
    )(parts)


def grads_kernel(agg, first_weight, sums, turned, term, hidden, out, first, second):
    first[...] = jnp.zeros_like(first)
    second[...] = term[...]

    def one_chunk(i, carry):
        at = pl.ds(pl.multiple_of(i * 2 * TILE, TILE), 2 * TILE)
        a = agg[at, :]
        v = jnp.dot(a, first_weight[...], preferred_element_type=F32)
        gate = 1.0 / (1.0 + jnp.exp(-v))
        h = (v * gate).astype(BF)
        hidden[at, :] = h
        grad_pre = turned[at, :].astype(F32) * gate * (1.0 + v * (1.0 - gate))
        first[...] += lax.dot_general(a, grad_pre.astype(BF), ROWS, preferred_element_type=F32)
        second[...] += lax.dot_general(h, sums[at, :], ROWS, preferred_element_type=F32)
        return carry

    lax.fori_loop(0, agg.shape[0] // (2 * TILE), one_chunk, 0)
    deep, wide = out.shape[2:]
    half = out.shape[1] // 2

    def one_band(i, carry):
        at = pl.ds(pl.multiple_of(i * deep, deep), deep)
        for n, source in enumerate((first, second)):
            for s in range(half):
                out[i, n * half + s] = source[at, s * wide : (s + 1) * wide].astype(BF)
        return carry

    lax.fori_loop(0, out.shape[0], one_band, 0)


def grads_step(agg, first_weight, sums, turned, term):
    rows, width = agg.shape
    return call(
        grads_kernel,
        (
            jax.ShapeDtypeStruct((rows, width), BF),
            jax.ShapeDtypeStruct((width // 16, 2 * width // 128, 16, 128), BF),
        ),
        [VMEM] * 5,
        [pltpu.VMEM((width, width), F32)] * 2,
        6 * rows * width * width,
        10 << 20,
        "grads_step",
    )(agg, first_weight, sums, turned, term)


def swap_sum(x, axis):
    got = lax.all_to_all(x, axis, split_axis=0, concat_axis=0, tiled=True)
    return jnp.sum(got.astype(F32), axis=0)


def share_out(x, axis, n):
    many = jnp.broadcast_to(x[None], (n, *x.shape))
    return lax.all_to_all(many, axis, split_axis=0, concat_axis=0, tiled=True)


def hop(x, axis, n, step):
    return lax.ppermute(x, axis, [(i, (i + step) % n) for i in range(n)])


def after(x, *others):
    return lax.optimization_barrier((x, *others))[0]


def add(*terms):
    return sum(t.astype(F32) for t in terms).astype(BF)


def shifts(parts, axis, n):
    return [parts[0]] + [hop(parts[t], axis, n, t) for t in range(1, n)]


def ring_reduce(block, z):
    half = RING // 2
    top, low = block(half)
    rows = top.shape[0]
    up = hop(top.astype(BF), "z", RING, 1)
    down = hop(low.astype(BF), "z", RING, -1)
    for s in range(half - 1, 0, -1):
        top, low = block(s)
        if s == half - 1:
            up = jnp.concatenate([top + up.astype(F32), low], axis=0).astype(BF)
            top, low = block(-s)
            down = jnp.concatenate([top, low + down.astype(F32)], axis=0).astype(BF)
        else:
            up = (jnp.concatenate([top, low], axis=0) + up.astype(F32)).astype(BF)
            down = (jnp.concatenate(block(-s), axis=0) + down.astype(F32)).astype(BF)
        up, down = hop(up, "z", RING, 1), hop(down, "z", RING, -1)
    return add(jnp.concatenate(block(0), axis=0), up, down)


def local(
    everyone,
    features,
    tile_data,
    tile_ids,
    tile_counts,
    hist_tiles,
    hist_ids,
    hist_cache,
    first_weight,
    second_weight,
    grad_out,
):
    share, width = features.shape
    scale = 1.0 / math.sqrt(share * everyone)
    core = lax.axis_index("core").astype(jnp.int32)
    z = lax.axis_index("z").astype(jnp.int32)
    y, x = (lax.axis_index(a).astype(jnp.int32) for a in ("y", "x"))
    where = jnp.stack([z, core, y, x])
    rows, panels = tile_data.shape[:2]

    numbers = jnp.concatenate([tile_ids, tile_counts[:, :, None]], axis=2)
    away = (1 - core) * (panels // 2)
    num_b = lax.ppermute(
        lax.dynamic_slice_in_dim(numbers, away, panels // 2, axis=1), "core", SWAP
    )
    tile_b = lax.ppermute(
        lax.dynamic_slice_in_dim(tile_data, away, panels // 2, axis=1), "core", SWAP
    )
    link = jnp.pad(hist_ids.T.astype(BF), ((0, 15), (0, TILE - rows)))
    link = jnp.concatenate([hist_tiles.reshape(rows * TILE, TILE), link], axis=0)

    rows_a = ring(features)
    rows_b = lax.ppermute(rows_a, "core", SWAP)
    operands = where, numbers, num_b, tile_data, tile_b
    chips = SIDE * SIDE
    first = back_product(
        first_back_kernel,
        jax.ShapeDtypeStruct((chips, share, width), BF),
        *operands,
        rows_a,
        rows_b,
    )
    first, grad_out, link = lax.optimization_barrier((first, grad_out, link))
    first = lax.all_to_all(first, ("y", "x"), split_axis=0, concat_axis=0, tiled=True)
    grad_a = ring(grad_out)
    grad_b = lax.ppermute(grad_a, "core", SWAP)
    links = shifts([link] * RING, "z", RING)
    link_ids = jnp.stack([piece[rows * TILE, :rows] for piece in links]).astype(jnp.int32)

    agg = agg_step(after(first, grad_b, *links[1:3], *links[6:]))
    agg = lax.all_to_all(agg, ("y", "x"), split_axis=0, concat_axis=0, tiled=True)
    square = jax.ShapeDtypeStruct((chips * share, width), BF)
    sums, turned = back_product(
        second_back_kernel, (square, square), *operands, grad_a, grad_b, second_weight
    )
    history, hist_term = hist_product(where, link_ids, hist_cache, grad_a, links)
    agg = after(agg.reshape(chips * share, width), sums, hist_term)
    pair, terms = grads_step(agg, first_weight, sums, turned, hist_term)
    sent = partner_product(where, num_b, tile_b, pair)
    taken = lax.ppermute(sent, "core", SWAP)
    terms = swap_sum(terms, ROW).astype(BF)
    term = lax.all_to_all(jnp.broadcast_to(terms[None], (RING, *terms.shape)), "z", 0, 0)
    term = (jnp.sum(term.astype(F32), axis=0) * scale).astype(BF)
    spread = share_out(term, ROW, everyone // RING)
    grads = spread.reshape(width // 16, 2 * width // 128, 16, 128).transpose(0, 2, 1, 3)
    grads = grads.reshape(width, 2 * width).astype(F32)
    kept = own_product(where, numbers, tile_data, pair, history)

    def block(offset):
        at = ((z + offset) & (RING - 1)) * share
        size = share // 2
        return [
            lax.dynamic_slice_in_dim(kept, at + n * size, size)
            + lax.dynamic_slice_in_dim(taken, at + n * size, size).astype(F32)
            for n in range(2)
        ]

    second_agg = ring_reduce(block, z)
    embedding = jnp.dot(second_agg, second_weight, preferred_element_type=F32).astype(BF)
    return (embedding, grads[:, :width], grads[:, width:])


def solution(mesh):
    chip_mesh = Mesh(mesh.devices.reshape(4, 4, 2, 8), ("y", "x", "core", "z"))
    placed = (
        P(ALL, None),
        P(ROW, "z", None, None, None),
        P(ROW, "z", None),
        P(ROW, "z"),
        P(ROW, "z", None, None),
        P(ROW, "z"),
        P("z", None),
        P(),
        P(),
        P(ALL, None),
    )
    return jax.shard_map(
        functools.partial(local, 256),
        mesh=chip_mesh,
        in_specs=placed,
        out_specs=(P(ALL, None), P(), P()),
        check_vma=False,
    )
```

```python
import functools
import math

import jax
import jax.numpy as jnp
from jax import lax
from jax.experimental import pallas as pl
from jax.experimental.pallas import tpu as pltpu
from jax.sharding import Mesh, PartitionSpec as P

BF = jnp.bfloat16
F32 = jnp.float32
TILE = 128
VMEM = pl.BlockSpec(memory_space=pltpu.VMEM)
SMEM = pl.BlockSpec(memory_space=pltpu.SMEM)
HBM = pl.BlockSpec(memory_space=pltpu.HBM)
ROWS = (((0,), (0,)), ((), ()))
COLS = (((1,), (1,)), ((), ()))
ROW = ("y", "x", "core")
ALL = ("y", "x", "core", "z")
SWAP = [(0, 1), (1, 0)]
RING = 8
SIDE = 4


def call(kernel, out_shape, specs, scratch, flops, moved, name, out_spec=VMEM):
    return pl.pallas_call(
        kernel,
        out_shape=out_shape,
        in_specs=specs,
        out_specs=jax.tree.map(lambda _: out_spec, out_shape),
        scratch_shapes=scratch,
        compiler_params=pltpu.CompilerParams(vmem_limit_bytes=24 << 20),
        cost_estimate=pl.CostEstimate(flops=flops, bytes_accessed=moved, transcendentals=0),
        name=name,
    )


def block_rows(index):
    return pl.ds(pl.multiple_of(index * TILE, TILE), TILE)


def ring_slot(source, mine):
    off = (source - mine) & (RING - 1)
    return jnp.where(off < RING // 2, 2 * off, 2 * RING - 1 - 2 * off)


def ring(x):
    up = [(i, (i + 1) % RING) for i in range(RING)]
    down = [(i, (i - 1) % RING) for i in range(RING)]
    half = x.shape[0] // 2
    pieces, u, d = [x], x, x
    for _ in range(RING // 2 - 1):
        u, d = lax.ppermute(u, "z", up), lax.ppermute(d, "z", down)
        pieces += [u, d]
    return pieces + [lax.ppermute(u[:half], "z", up), lax.ppermute(d[half:], "z", down)]


def back_sums(where, num_a, num_b, tile_a, tile_b, src_a, src_b, total):
    z, core = where[0], where[1]
    rows, panels, slots = tile_b.shape[:3]
    columns = total.shape[0] // panels // TILE
    total[...] = jnp.zeros_like(total)
    for num, tiles, src, first in (
        (num_a, tile_a, src_a, panels * core),
        (num_b, tile_b, src_b, 0),
    ):

        def one_row(i, carry):
            block = src[block_rows(ring_slot(i, z)), :]
            parts = []
            for j in range(panels):
                used = num[i, first + j, slots]
                for t in range(slots):
                    tile = tiles[i, first + j, t]
                    tile = jnp.where(t < used, tile, jnp.zeros_like(tile))
                    part = lax.dot_general(tile, block, ROWS, preferred_element_type=F32)
                    parts.append((j * columns + num[i, first + j, t], part))
            for place, part in parts:
                total[block_rows(place), :] += part
            return carry

        lax.fori_loop(0, rows, one_row, 0, unroll=2)


def first_back_kernel(*refs):
    out, total, rounded, sems = refs[-4:]
    back_sums(*refs[:-4], total)
    copies = []
    for a in range(out.shape[0]):
        rounded[a] = total[pl.ds(a * TILE, TILE), :].astype(BF)
        copies.append(pltpu.make_async_copy(rounded.at[a], out.at[a], sems.at[a]))
        copies[-1].start()
    for copy in copies:
        copy.wait()


def second_back_kernel(*refs):
    weight, out, turned, total = refs[7:]
    back_sums(*refs[:7], total)

    def one_chunk(i, carry):
        at = pl.ds(pl.multiple_of(i * 4 * TILE, TILE), 4 * TILE)
        value = total[at, :].astype(BF)
        out[at, :] = value
        part = lax.dot_general(value, weight[...], COLS, preferred_element_type=F32)
        turned[at, :] = part.astype(BF)
        return carry

    lax.fori_loop(0, total.shape[0] // (4 * TILE), one_chunk, 0)


def back_product(kernel, out_shape, scratch, out_spec, *operands):
    rows, panels, slots = operands[4].shape[:3]
    height, width = panels * 8 * TILE, operands[5].shape[1]
    return call(
        kernel,
        out_shape,
        [SMEM] * 3 + [VMEM] * (len(operands) - 3),
        [pltpu.VMEM((height, width), F32), *scratch],
        4 * rows * panels * slots * TILE * TILE * width,
        8 << 20,
        "back_product",
        out_spec,
    )(*operands)


def row_blocks(where, num, tiles, source, first, start, out):
    rows, _, slots = tiles.shape[:3]
    panels = 2
    columns = source.shape[0] // panels // TILE

    def one_row(i, carry):
        at = block_rows(i)
        acc = start[at, :] if start is not None else jnp.zeros((TILE, out.shape[1]), F32)
        for j in range(panels):
            used = num[i, first + j, slots]
            for t in range(slots):
                tile = tiles[i, first + j, t]
                tile = jnp.where(t < used, tile, jnp.zeros_like(tile))
                part = source[block_rows(j * columns + num[i, first + j, t]), :]
                acc += jnp.dot(tile, part, preferred_element_type=F32)
        out[at, :] = acc.astype(out.dtype)
        return carry

    lax.fori_loop(0, rows, one_row, 0, unroll=2)


def partner_kernel(where, num, tiles, pair, out):
    row_blocks(where, num, tiles, pair, 0, None, out)


def own_kernel(where, num, tiles, pair, history, out):
    row_blocks(where, num, tiles, pair, 2 * where[1], history, out)


def partner_product(where, num, tiles, pair):
    rows, width = tiles.shape[0], pair.shape[1]
    return call(
        partner_kernel,
        jax.ShapeDtypeStruct((rows * TILE, width), BF),
        [SMEM] * 2 + [VMEM] * 2,
        [],
        8 * rows * TILE * TILE * width,
        4 << 20,
        "row_product",
    )(where, num, tiles, pair)


def own_product(where, num, tiles, pair, history):
    rows, width = tiles.shape[0], pair.shape[1]
    return call(
        own_kernel,
        jax.ShapeDtypeStruct((rows * TILE, width), F32),
        [SMEM] * 2 + [VMEM] * 3,
        [],
        8 * rows * TILE * TILE * width,
        5 << 20,
        "row_product",
    )(where, num, tiles, pair, history)


def hist_kernel(where, ids, cache, *refs):
    pieces, (out, term, held, sems) = refs[:-4], refs[-4:]
    share = pieces[-1].shape[0]
    spots = [held.at[n] for n in range(RING - 1)]
    spots += [held.at[RING - 1, pl.ds(n * share, share), :] for n in range(2)]
    copies = [
        pltpu.make_async_copy(piece, spot, sems.at[n])
        for n, (piece, spot) in enumerate(zip(pieces, spots))
    ]
    for copy in copies:
        copy.start()
    blocks = cache.shape[0] // TILE
    z = where[0]
    rows = ids.shape[1]
    lanes = out.shape[1] // TILE
    out[...] = jnp.zeros_like(out)
    term[...] = jnp.zeros_like(term)
    for copy in copies:
        copy.wait()

    def one_piece(n, carry):
        for p in range(rows):
            block = ids[n, p] - z * blocks

            @pl.when((block >= 0) & (block < blocks))
            def _():
                tile = held[
                    n,
                    (1 + p // lanes) * TILE : (2 + p // lanes) * TILE,
                    (p % lanes) * TILE : (p % lanes + 1) * TILE,
                ]
                out[p * TILE : (p + 1) * TILE, :] += jnp.dot(
                    tile, cache[block_rows(block), :], preferred_element_type=F32
                )

        return carry

    lax.fori_loop(0, RING, one_piece, 0)

    def one_term(p, carry):
        term[...] += lax.dot_general(
            out[block_rows(p), :].astype(BF),
            held[ring_slot(p, z), :TILE, :],
            ROWS,
            preferred_element_type=F32,
        )
        return carry

    lax.fori_loop(0, rows, one_term, 0)


def hist_product(where, ids, cache, pieces):
    rows, width = ids.shape[1], cache.shape[1]
    return call(
        hist_kernel,
        (
            jax.ShapeDtypeStruct((rows * TILE, width), F32),
            jax.ShapeDtypeStruct((width, width), F32),
        ),
        [SMEM] * 2 + [VMEM] + [HBM] * len(pieces),
        [
            pltpu.VMEM((RING, *pieces[0].shape), BF),
            pltpu.SemaphoreType.DMA((len(pieces),)),
        ],
        2 * rows * TILE * TILE * width + 2 * rows * TILE * width * width,
        6 << 20,
        "hist_product",
    )(where, ids, cache, *pieces)


def agg_kernel(parts, out, total, sems):
    value = parts[0].astype(F32)
    for i in range(1, parts.shape[0]):
        value += parts[i].astype(F32)
    total[...] = value.astype(BF)
    copies = [
        pltpu.make_async_copy(total, out.at[i], sems.at[i]) for i in range(out.shape[0])
    ]
    for copy in copies:
        copy.start()
    for copy in copies:
        copy.wait()


def agg_step(parts):
    return call(
        agg_kernel,
        jax.ShapeDtypeStruct(parts.shape, BF),
        [VMEM],
        [pltpu.VMEM(parts.shape[1:], BF), pltpu.SemaphoreType.DMA((parts.shape[0],))],
        parts.size,
        4 << 20,
        "agg_step",
        HBM,
    )(parts)


def grads_kernel(agg, first_weight, sums, turned, term, hidden, out, first, second):
    first[...] = jnp.zeros_like(first)
    second[...] = term[...]

    def one_chunk(i, carry):
        at = pl.ds(pl.multiple_of(i * 2 * TILE, TILE), 2 * TILE)
        a = agg[at, :]
        v = jnp.dot(a, first_weight[...], preferred_element_type=F32)
        gate = 1.0 / (1.0 + jnp.exp(-v))
        h = (v * gate).astype(BF)
        hidden[at, :] = h
        grad_pre = turned[at, :].astype(F32) * gate * (1.0 + v * (1.0 - gate))
        first[...] += lax.dot_general(a, grad_pre.astype(BF), ROWS, preferred_element_type=F32)
        second[...] += lax.dot_general(h, sums[at, :], ROWS, preferred_element_type=F32)
        return carry

    lax.fori_loop(0, agg.shape[0] // (2 * TILE), one_chunk, 0)
    deep, wide = out.shape[2:]
    half = out.shape[1] // 2

    def one_band(i, carry):
        at = pl.ds(pl.multiple_of(i * deep, deep), deep)
        for n, source in enumerate((first, second)):
            for s in range(half):
                out[i, n * half + s] = source[at, s * wide : (s + 1) * wide].astype(BF)
        return carry

    lax.fori_loop(0, out.shape[0], one_band, 0)


def grads_step(agg, first_weight, sums, turned, term):
    rows, width = agg.shape
    return call(
        grads_kernel,
        (
            jax.ShapeDtypeStruct((rows, width), BF),
            jax.ShapeDtypeStruct((width // 16, 2 * width // 128, 16, 128), BF),
        ),
        [VMEM] * 5,
        [pltpu.VMEM((width, width), F32)] * 2,
        6 * rows * width * width,
        10 << 20,
        "grads_step",
    )(agg, first_weight, sums, turned, term)


def swap_sum(x, axis):
    got = lax.all_to_all(x, axis, split_axis=0, concat_axis=0, tiled=True)
    return jnp.sum(got.astype(F32), axis=0)


def share_out(x, axis, n):
    many = jnp.broadcast_to(x[None], (n, *x.shape))
    return lax.all_to_all(many, axis, split_axis=0, concat_axis=0, tiled=True)


def hop(x, axis, n, step):
    return lax.ppermute(x, axis, [(i, (i + step) % n) for i in range(n)])


def after(x, *others):
    return lax.optimization_barrier((x, *others))[0]


def add(*terms):
    return sum(t.astype(F32) for t in terms).astype(BF)


def shifts(parts, axis, n):
    return [parts[0]] + [hop(parts[t], axis, n, t) for t in range(1, n)]


def ring_reduce(block, z):
    half = RING // 2
    top, low = block(half)
    rows = top.shape[0]
    up = hop(top.astype(BF), "z", RING, 1)
    down = hop(low.astype(BF), "z", RING, -1)
    for s in range(half - 1, 0, -1):
        top, low = block(s)
        if s == half - 1:
            up = jnp.concatenate([top + up.astype(F32), low], axis=0).astype(BF)
            top, low = block(-s)
            down = jnp.concatenate([top, low + down.astype(F32)], axis=0).astype(BF)
        else:
            up = (jnp.concatenate([top, low], axis=0) + up.astype(F32)).astype(BF)
            down = (jnp.concatenate(block(-s), axis=0) + down.astype(F32)).astype(BF)
        up, down = hop(up, "z", RING, 1), hop(down, "z", RING, -1)
    return add(jnp.concatenate(block(0), axis=0), up, down)


def local(
    everyone,
    features,
    tile_data,
    tile_ids,
    tile_counts,
    hist_tiles,
    hist_ids,
    hist_cache,
    first_weight,
    second_weight,
    grad_out,
):
    share, width = features.shape
    scale = 1.0 / math.sqrt(share * everyone)
    core = lax.axis_index("core").astype(jnp.int32)
    z = lax.axis_index("z").astype(jnp.int32)
    y, x = (lax.axis_index(a).astype(jnp.int32) for a in ("y", "x"))
    where = jnp.stack([z, core, y, x])
    rows, panels = tile_data.shape[:2]

    numbers = jnp.concatenate([tile_ids, tile_counts[:, :, None]], axis=2)
    away = (1 - core) * (panels // 2)
    num_b = lax.ppermute(
        lax.dynamic_slice_in_dim(numbers, away, panels // 2, axis=1), "core", SWAP
    )
    tile_b = lax.ppermute(
        lax.dynamic_slice_in_dim(tile_data, away, panels // 2, axis=1), "core", SWAP
    )
    lanes = width // TILE
    link = hist_tiles.reshape(rows // lanes, lanes, TILE, TILE).transpose(0, 2, 1, 3)
    marks = jnp.pad(hist_ids.T.astype(BF), ((0, 31), (0, width - rows)))
    load = jnp.concatenate([grad_out, link.reshape(-1, width), marks], axis=0)

    rows_a = jnp.concatenate(ring(features), axis=0)
    rows_b = lax.ppermute(rows_a, "core", SWAP)
    operands = where, numbers, num_b, tile_data, tile_b
    chips = SIDE * SIDE
    stack = (chips, share, width)
    first = back_product(
        first_back_kernel,
        jax.ShapeDtypeStruct(stack, BF),
        [pltpu.VMEM(stack, BF), pltpu.SemaphoreType.DMA((chips,))],
        HBM,
        *operands,
        rows_a,
        rows_b,
    )
    first, load = lax.optimization_barrier((first, load))
    first = lax.all_to_all(first, ("y", "x"), split_axis=0, concat_axis=0, tiled=True)
    pieces = ring(load)
    agg = agg_step(after(first, *pieces[-2:]))
    agg = lax.all_to_all(agg, ("y", "x"), split_axis=0, concat_axis=0, tiled=True)
    grad_a = jnp.concatenate([piece[:share] for piece in pieces[:RING]], axis=0)
    grad_b = lax.ppermute(grad_a, "core", SWAP)
    mark = 3 * share
    marks = [piece[mark, :rows] for piece in pieces[: RING - 1]]
    marks += [pieces[-1][mark - pieces[-1].shape[0], :rows]]
    history, hist_term = hist_product(
        where, jnp.stack(marks).astype(jnp.int32), hist_cache, pieces
    )
    square = jax.ShapeDtypeStruct((chips * share, width), BF)
    sums, turned = back_product(
        second_back_kernel,
        (square, square),
        [],
        VMEM,
        *operands,
        grad_a,
        grad_b,
        second_weight,
    )
    agg = after(agg.reshape(chips * share, width), sums, hist_term)
    pair, terms = grads_step(agg, first_weight, sums, turned, hist_term)
    sent = partner_product(where, num_b, tile_b, pair)
    taken = lax.ppermute(sent, "core", SWAP)
    terms = swap_sum(terms, ROW).astype(BF)
    term = lax.all_to_all(jnp.broadcast_to(terms[None], (RING, *terms.shape)), "z", 0, 0)
    term = (jnp.sum(term.astype(F32), axis=0) * scale).astype(BF)
    spread = share_out(term, ROW, everyone // RING)
    grads = spread.reshape(width // 16, 2 * width // 128, 16, 128).transpose(0, 2, 1, 3)
    grads = grads.reshape(width, 2 * width).astype(F32)
    kept = own_product(where, numbers, tile_data, pair, history)

    def block(offset):
        at = ((z + offset) & (RING - 1)) * share
        size = share // 2
        return [
            lax.dynamic_slice_in_dim(kept, at + n * size, size)
            + lax.dynamic_slice_in_dim(taken, at + n * size, size).astype(F32)
            for n in range(2)
        ]

    second_agg = ring_reduce(block, z)
    embedding = jnp.dot(second_agg, second_weight, preferred_element_type=F32).astype(BF)
    return (embedding, grads[:, :width], grads[:, width:])


def solution(mesh):
    chip_mesh = Mesh(mesh.devices.reshape(4, 4, 2, 8), ("y", "x", "core", "z"))
    placed = (
        P(ALL, None),
        P(ROW, "z", None, None, None),
        P(ROW, "z", None),
        P(ROW, "z"),
        P(ROW, "z", None, None),
        P(ROW, "z"),
        P("z", None),
        P(),
        P(),
        P(ALL, None),
    )
    return jax.shard_map(
        functools.partial(local, 256),
        mesh=chip_mesh,
        in_specs=placed,
        out_specs=(P(ALL, None), P(), P()),
        check_vma=False,
    )
```

```python
import functools
import math

import jax
import jax.numpy as jnp
from jax import lax
from jax.experimental import pallas as pl
from jax.experimental.pallas import tpu as pltpu
from jax.sharding import Mesh, PartitionSpec as P

BF = jnp.bfloat16
F32 = jnp.float32
TILE = 128
VMEM = pl.BlockSpec(memory_space=pltpu.VMEM)
SMEM = pl.BlockSpec(memory_space=pltpu.SMEM)
ROWS = (((0,), (0,)), ((), ()))
COLS = (((1,), (1,)), ((), ()))
ROW = ("y", "x", "core")
ALL = ("y", "x", "core", "z")
SWAP = [(0, 1), (1, 0)]
RING = 8
SIDE = 4


def call(kernel, out_shape, specs, scratch, flops, moved, name):
    return pl.pallas_call(
        kernel,
        out_shape=out_shape,
        in_specs=specs,
        out_specs=jax.tree.map(lambda _: VMEM, out_shape),
        scratch_shapes=scratch,
        compiler_params=pltpu.CompilerParams(vmem_limit_bytes=24 << 20),
        cost_estimate=pl.CostEstimate(flops=flops, bytes_accessed=moved, transcendentals=0),
        name=name,
    )


def block_rows(index):
    return pl.ds(pl.multiple_of(index * TILE, TILE), TILE)


def ring_slot(source, mine):
    off = (source - mine) & (RING - 1)
    return jnp.where(off < RING // 2, 2 * off, 2 * RING - 1 - 2 * off)


def ring(x):
    up = [(i, (i + 1) % RING) for i in range(RING)]
    down = [(i, (i - 1) % RING) for i in range(RING)]
    half = x.shape[0] // 2
    pieces, u, d = [x], x, x
    for _ in range(RING // 2 - 1):
        u, d = lax.ppermute(u, "z", up), lax.ppermute(d, "z", down)
        pieces += [u, d]
    return pieces + [lax.ppermute(u[:half], "z", up), lax.ppermute(d[half:], "z", down)]


def back_sums(where, num_a, num_b, tile_a, tile_b, src_a, src_b, total):
    z, core = where[0], where[1]
    rows, panels, slots = tile_b.shape[:3]
    columns = total.shape[0] // panels // TILE
    stride = src_a.shape[0] // RING
    total[...] = jnp.zeros_like(total)
    for num, tiles, src, first in (
        (num_a, tile_a, src_a, panels * core),
        (num_b, tile_b, src_b, 0),
    ):

        def one_row(i, carry):
            spot = pl.multiple_of(ring_slot(i, z) * stride, stride & -stride)
            block = src[pl.ds(spot, TILE), :]
            parts = []
            for j in range(panels):
                used = num[i, first + j, slots]
                for t in range(slots):
                    tile = tiles[i, first + j, t]
                    tile = jnp.where(t < used, tile, jnp.zeros_like(tile))
                    part = lax.dot_general(tile, block, ROWS, preferred_element_type=F32)
                    parts.append((j * columns + num[i, first + j, t], part))
            for place, part in parts:
                total[block_rows(place), :] += part
            return carry

        lax.fori_loop(0, rows, one_row, 0, unroll=2)


def first_back_kernel(*refs):
    out, total = refs[-2:]
    back_sums(*refs[:-2], total)
    for a in range(out.shape[0]):
        out[a] = total[pl.ds(a * TILE, TILE), :].astype(BF)


def second_back_kernel(*refs):
    weight, out, turned, total = refs[7:]
    back_sums(*refs[:7], total)

    def one_chunk(i, carry):
        at = pl.ds(pl.multiple_of(i * 4 * TILE, TILE), 4 * TILE)
        value = total[at, :].astype(BF)
        out[at, :] = value
        part = lax.dot_general(value, weight[...], COLS, preferred_element_type=F32)
        turned[at, :] = part.astype(BF)
        return carry

    lax.fori_loop(0, total.shape[0] // (4 * TILE), one_chunk, 0)


def back_product(kernel, out_shape, *operands):
    rows, panels, slots = operands[4].shape[:3]
    height, width = panels * 8 * TILE, operands[5].shape[1]
    return call(
        kernel,
        out_shape,
        [SMEM] * 3 + [VMEM] * (len(operands) - 3),
        [pltpu.VMEM((height, width), F32)],
        4 * rows * panels * slots * TILE * TILE * width,
        8 << 20,
        "back_product",
    )(*operands)


def row_blocks(where, num, tiles, source, first, start, out):
    rows, _, slots = tiles.shape[:3]
    panels = 2
    columns = source.shape[0] // panels // TILE

    def one_row(i, carry):
        at = block_rows(i)
        acc = start[at, :] if start is not None else jnp.zeros((TILE, out.shape[1]), F32)
        for j in range(panels):
            used = num[i, first + j, slots]
            for t in range(slots):
                tile = tiles[i, first + j, t]
                tile = jnp.where(t < used, tile, jnp.zeros_like(tile))
                part = source[block_rows(j * columns + num[i, first + j, t]), :]
                acc += jnp.dot(tile, part, preferred_element_type=F32)
        out[at, :] = acc.astype(out.dtype)
        return carry

    lax.fori_loop(0, rows, one_row, 0, unroll=2)


def row_kernel(where, num_a, num_b, tile_a, tile_b, pair, history, sent, kept):
    row_blocks(where, num_b, tile_b, pair, 0, None, sent)
    row_blocks(where, num_a, tile_a, pair, 2 * where[1], history, kept)


def row_product(where, num_a, num_b, tile_a, tile_b, pair, history):
    rows, width = tile_b.shape[0], pair.shape[1]
    return call(
        row_kernel,
        (
            jax.ShapeDtypeStruct((rows * TILE, width), BF),
            jax.ShapeDtypeStruct((rows * TILE, width), F32),
        ),
        [SMEM] * 3 + [VMEM] * 4,
        [],
        16 * rows * TILE * TILE * width,
        9 << 20,
        "row_product",
    )(where, num_a, num_b, tile_a, tile_b, pair, history)


def hist_kernel(lead, where, ids, cache, *refs):
    pieces, (out, term, last) = refs[:-3], refs[-3:]
    share = pieces[-1].shape[0]
    last[:share, :] = pieces[-2][...]
    last[share:, :] = pieces[-1][...]
    held = [*pieces[:-2], last]
    blocks = cache.shape[0] // TILE
    z = where[0]
    rows = ids.shape[1]
    lanes = out.shape[1] // TILE
    out[...] = jnp.zeros_like(out)
    for n, piece in enumerate(held):

        def one_row(p, carry):
            block = ids[n, p] - z * blocks

            @pl.when((block >= 0) & (block < blocks))
            def _():
                high = pl.multiple_of(lead + (p // lanes) * TILE, lead & -lead)
                wide = pl.multiple_of((p & (lanes - 1)) * TILE, TILE)
                out[block_rows(p), :] += jnp.dot(
                    piece[pl.ds(high, TILE), pl.ds(wide, TILE)],
                    cache[block_rows(block), :],
                    preferred_element_type=F32,
                )

            return carry

        lax.fori_loop(0, rows, one_row, 0)
    term[...] = jnp.zeros_like(term)
    for n, piece in enumerate(held):
        source = (z + (0, -1, 1, -2, 2, -3, 3, 4)[n]) & (RING - 1)
        term[...] += lax.dot_general(
            out[block_rows(source), :].astype(BF),
            piece[:TILE, :],
            ROWS,
            preferred_element_type=F32,
        )


def hist_product(lead, where, ids, cache, pieces):
    rows, width = ids.shape[1], cache.shape[1]
    return call(
        functools.partial(hist_kernel, lead),
        (
            jax.ShapeDtypeStruct((rows * TILE, width), F32),
            jax.ShapeDtypeStruct((width, width), F32),
        ),
        [SMEM] * 2 + [VMEM] * (1 + len(pieces)),
        [pltpu.VMEM(pieces[0].shape, BF)],
        2 * rows * TILE * TILE * width + 2 * rows * TILE * width * width,
        6 << 20,
        "hist_product",
    )(where, ids, cache, *pieces)


def agg_kernel(parts, out):
    total = parts[0].astype(F32)
    for i in range(1, parts.shape[0]):
        total += parts[i].astype(F32)
    total = total.astype(BF)
    for i in range(out.shape[0]):
        out[i] = total


def agg_step(parts):
    return call(
        agg_kernel,
        jax.ShapeDtypeStruct(parts.shape, BF),
        [VMEM],
        [],
        parts.size,
        4 << 20,
        "agg_step",
    )(parts)


def grads_kernel(agg, first_weight, sums, turned, term, hidden, out, first, second):
    first[...] = jnp.zeros_like(first)
    second[...] = term[...]

    def one_chunk(i, carry):
        at = pl.ds(pl.multiple_of(i * 2 * TILE, TILE), 2 * TILE)
        a = agg[at, :]
        v = jnp.dot(a, first_weight[...], preferred_element_type=F32)
        gate = 1.0 / (1.0 + jnp.exp(-v))
        h = (v * gate).astype(BF)
        hidden[at, :] = h
        grad_pre = turned[at, :].astype(F32) * gate * (1.0 + v * (1.0 - gate))
        first[...] += lax.dot_general(a, grad_pre.astype(BF), ROWS, preferred_element_type=F32)
        second[...] += lax.dot_general(h, sums[at, :], ROWS, preferred_element_type=F32)
        return carry

    lax.fori_loop(0, agg.shape[0] // (2 * TILE), one_chunk, 0)
    deep, wide = out.shape[2:]
    half = out.shape[1] // 2

    def one_band(i, carry):
        at = pl.ds(pl.multiple_of(i * deep, deep), deep)
        for n, source in enumerate((first, second)):
            for s in range(half):
                out[i, n * half + s] = source[at, s * wide : (s + 1) * wide].astype(BF)
        return carry

    lax.fori_loop(0, out.shape[0], one_band, 0)


def grads_step(agg, first_weight, sums, turned, term):
    rows, width = agg.shape
    return call(
        grads_kernel,
        (
            jax.ShapeDtypeStruct((rows, width), BF),
            jax.ShapeDtypeStruct((width // 16, 2 * width // 128, 16, 128), BF),
        ),
        [VMEM] * 5,
        [pltpu.VMEM((width, width), F32)] * 2,
        6 * rows * width * width,
        10 << 20,
        "grads_step",
    )(agg, first_weight, sums, turned, term)


def swap_sum(x, axis):
    got = lax.all_to_all(x, axis, split_axis=0, concat_axis=0, tiled=True)
    return jnp.sum(got.astype(F32), axis=0)


def share_out(x, axis, n):
    many = jnp.broadcast_to(x[None], (n, *x.shape))
    return lax.all_to_all(many, axis, split_axis=0, concat_axis=0, tiled=True)


def hop(x, axis, n, step):
    return lax.ppermute(x, axis, [(i, (i + step) % n) for i in range(n)])


def after(x, *others):
    return lax.optimization_barrier((x, *others))[0]


def add(*terms):
    return sum(t.astype(F32) for t in terms).astype(BF)


def shifts(parts, axis, n):
    return [parts[0]] + [hop(parts[t], axis, n, t) for t in range(1, n)]


def ring_reduce(block, z):
    half = RING // 2
    top, low = block(half)
    rows = top.shape[0]
    up = hop(top.astype(BF), "z", RING, 1)
    down = hop(low.astype(BF), "z", RING, -1)
    for s in range(half - 1, 0, -1):
        top, low = block(s)
        if s == half - 1:
            up = jnp.concatenate([top + up.astype(F32), low], axis=0).astype(BF)
            top, low = block(-s)
            down = jnp.concatenate([top, low + down.astype(F32)], axis=0).astype(BF)
        else:
            up = (jnp.concatenate([top, low], axis=0) + up.astype(F32)).astype(BF)
            down = (jnp.concatenate(block(-s), axis=0) + down.astype(F32)).astype(BF)
        up, down = hop(up, "z", RING, 1), hop(down, "z", RING, -1)
    return add(jnp.concatenate(block(0), axis=0), up, down)


def local(
    everyone,
    features,
    tile_data,
    tile_ids,
    tile_counts,
    hist_tiles,
    hist_ids,
    hist_cache,
    first_weight,
    second_weight,
    grad_out,
):
    share, width = features.shape
    scale = 1.0 / math.sqrt(share * everyone)
    core = lax.axis_index("core").astype(jnp.int32)
    z = lax.axis_index("z").astype(jnp.int32)
    y, x = (lax.axis_index(a).astype(jnp.int32) for a in ("y", "x"))
    where = jnp.stack([z, core, y, x])
    rows, panels = tile_data.shape[:2]

    numbers = jnp.concatenate([tile_ids, tile_counts[:, :, None]], axis=2)
    away = (1 - core) * (panels // 2)
    num_b = lax.ppermute(
        lax.dynamic_slice_in_dim(numbers, away, panels // 2, axis=1), "core", SWAP
    )
    tile_b = lax.ppermute(
        lax.dynamic_slice_in_dim(tile_data, away, panels // 2, axis=1), "core", SWAP
    )
    lanes = width // TILE
    link = hist_tiles.reshape(rows // lanes, lanes, TILE, TILE).transpose(0, 2, 1, 3)
    marks = jnp.pad(hist_ids.T.astype(BF), ((0, 31), (0, width - rows)))
    load = jnp.concatenate([grad_out, marks, link.reshape(-1, width)], axis=0)
    lead = share + marks.shape[0]

    rows_a = jnp.concatenate(ring(features), axis=0)
    rows_b = lax.ppermute(rows_a, "core", SWAP)
    operands = where, numbers, num_b, tile_data, tile_b
    chips = SIDE * SIDE
    stack = (chips, share, width)
    first = back_product(
        first_back_kernel,
        jax.ShapeDtypeStruct(stack, BF),
        *operands,
        rows_a,
        rows_b,
    )
    first, load = lax.optimization_barrier((first, load))
    first = lax.all_to_all(first, ("y", "x"), split_axis=0, concat_axis=0, tiled=True)
    pieces = ring(load)
    agg = agg_step(after(first, *pieces[5:7]))
    agg = lax.all_to_all(agg, ("y", "x"), split_axis=0, concat_axis=0, tiled=True)
    grad_a = jnp.concatenate([piece[:lead] for piece in pieces[:RING]], axis=0)
    grad_b = lax.ppermute(grad_a, "core", SWAP)
    link_ids = grad_a.reshape(RING, lead, width)[:, share, :rows].astype(jnp.int32)
    history, hist_term = hist_product(lead, where, link_ids, hist_cache, pieces)
    square = jax.ShapeDtypeStruct((chips * share, width), BF)
    sums, turned = back_product(
        second_back_kernel,
        (square, square),
        *operands,
        grad_a,
        grad_b,
        second_weight,
    )
    agg = agg.reshape(chips * share, width)
    pair, terms = grads_step(agg, first_weight, sums, turned, hist_term)
    sent, kept = row_product(*operands, pair, history)
    taken = lax.ppermute(sent, "core", SWAP)
    terms = swap_sum(terms, ROW).astype(BF)
    term = lax.all_to_all(jnp.broadcast_to(terms[None], (RING, *terms.shape)), "z", 0, 0)
    term = (jnp.sum(term.astype(F32), axis=0) * scale).astype(BF)
    spread = share_out(term, ROW, everyone // RING)
    grads = spread.reshape(width // 16, 2 * width // 128, 16, 128).transpose(0, 2, 1, 3)
    grads = grads.reshape(width, 2 * width).astype(F32)

    def block(offset):
        at = ((z + offset) & (RING - 1)) * share
        size = share // 2
        return [
            lax.dynamic_slice_in_dim(kept, at + n * size, size)
            + lax.dynamic_slice_in_dim(taken, at + n * size, size).astype(F32)
            for n in range(2)
        ]

    second_agg = ring_reduce(block, z)
    embedding = jnp.dot(second_agg, second_weight, preferred_element_type=F32).astype(BF)
    return (embedding, grads[:, :width], grads[:, width:])


def solution(mesh):
    chip_mesh = Mesh(mesh.devices.reshape(4, 4, 2, 8), ("y", "x", "core", "z"))
    placed = (
        P(ALL, None),
        P(ROW, "z", None, None, None),
        P(ROW, "z", None),
        P(ROW, "z"),
        P(ROW, "z", None, None),
        P(ROW, "z"),
        P("z", None),
        P(),
        P(),
        P(ALL, None),
    )
    return jax.shard_map(
        functools.partial(local, 256),
        mesh=chip_mesh,
        in_specs=placed,
        out_specs=(P(ALL, None), P(), P()),
        check_vma=False,
    )
```
